32 devices in a mesh: segment: 4 (over z), ctx: 2 (over x), dp: 4 (over y, core).
Axes of the slice: x: 2, y: 2, z: 4, core: 2. Of those that a mesh axis runs over, the one named last changes fastest.
Arguments:
- qkv: bfloat16 [4, 4, 320, 3, 2560], P('segment', 'dp', 'ctx'), may hold values from -24 to 24
- qk_gain: float32 [4, 2, 2560], P('segment'), may hold values from 1.5 to 2.5
- mod_weight: float32 [4, 256, 2560], P('segment'), may hold values from -0.375 to 0.375
- positions: int32 [4, 320], P('dp', 'ctx'), may hold values from 0 to 75599
- timesteps: int32 [4, 4], P('segment', 'dp'), may hold values from 0 to 999
- cotangent: bfloat16 [4, 4, 320, 2560], P('segment', 'dp', 'ctx'), may hold values from -6 to 6
Outputs:
- attn_out: bfloat16 [4, 4, 320, 2560], P('segment', 'dp', 'ctx')
- gate_grad: float32 [4, 256, 2560], P('segment', ('ctx', 'dp'))
The draws below stay inside these ranges and needn't reach their ends.
All inputs are finite; a program needn't handle non-finite values.
Results may differ from the reference program's by a relative error of at most 0.012.
Values may be sent and summed in bfloat16 or wider, within the bound.
A program may use at most 128 MiB of HBM per device.

```python
import jax
import jax.numpy as jnp
from jax import lax

HEADS = 20
HEAD_DIM = 128
FREQS = 256
GRID_ROWS = 45
GRID_COLS = 80
FRAMES = 21
STEPS = 1000
TOKENS = 320
HW = 2560
N_SEGMENT = 4
N_DP = 4


def draw_qkv(key, part):
    width = HEADS * HEAD_DIM
    shape = (N_SEGMENT, N_DP, TOKENS, 3, width)
    streams = jax.random.split(jax.random.fold_in(key, 11), 1)
    base = jax.random.normal(streams[0], shape, jnp.float32)
    return jnp.clip(base, -24.0, 24.0).astype(jnp.bfloat16)


def with_ends(values, key, low, largest):
    index_at = [jax.random.randint(jax.random.fold_in(key, axis), (), 0, length) for axis, length in enumerate(values.shape)]
    main_axis = values.shape.index(max(values.shape))
    next_to = index_at[:main_axis] + [(index_at[main_axis] + 1) % values.shape[main_axis]] + index_at[main_axis + 1:]
    return values.at[tuple(index_at)].set(low).at[tuple(next_to)].set(largest)


def shard_levels(stream_key, shape, shards, least, high):
    level, own = 1.0, jax.random.fold_in(stream_key, 6)
    for axis_at, parts in shards:
        heights = jnp.exp(jax.random.uniform(jax.random.fold_in(own, axis_at), (parts,), jnp.float32, least / len(shards), high / len(shards)))
        level = level * jnp.repeat(heights, shape[axis_at] // parts).reshape([-1 if axis == axis_at else 1 for axis in range(len(shape))])
    return level


def bell_draw(key, extent, scale, most, cuts=(), kind=jnp.bfloat16):
    values = jax.random.normal(key, extent, jnp.float32) * scale
    if len(cuts) > 0:
        values = shard_levels(key, extent, cuts, -0.22, 0.18) * values
    return jnp.clip(values, min=-most, max=most).astype(kind)


def setup_inputs(seed: int = 0) -> dict:
    arg_keys = jax.random.split(jax.random.key(seed), 7)
    qkv = draw_qkv(jax.random.fold_in(arg_keys[6], 71), 0)
    qk_gain = jnp.clip(1.5 + 1.0 * jax.random.uniform(arg_keys[1], (N_SEGMENT, 2, HW), jnp.float32) ** shard_levels(arg_keys[1], (N_SEGMENT, 2, HW), ((0, 4),), -0.2, 0.2), 1.5, 2.5)
    mod_weight = bell_draw(arg_keys[2], (N_SEGMENT, FREQS, HW), FREQS ** -0.5, 0.375, ((0, 4),), jnp.float32)
    positions = with_ends(jax.random.randint(arg_keys[3], (N_DP, TOKENS), 0, FRAMES * GRID_ROWS * GRID_COLS), jax.random.fold_in(arg_keys[3], 1), 0, (FRAMES * GRID_ROWS * GRID_COLS) - 1).astype(jnp.int32)
    timesteps = with_ends(jax.random.randint(arg_keys[4], (N_SEGMENT, N_DP), 0, STEPS), jax.random.fold_in(arg_keys[4], 1), 0, STEPS - 1).astype(jnp.int32)
    cotangent = bell_draw(arg_keys[5], (N_SEGMENT, N_DP, TOKENS, HW), 1.0, 6.0, ((0, 4), (1, 4), (2, 2)))
    return {"qkv": qkv, "qk_gain": qk_gain, "mod_weight": mod_weight, "positions": positions, "timesteps": timesteps, "cotangent": cotangent}


def rope_tables(pos):
    half = HEAD_DIM // 2
    side = HEAD_DIM // 6
    first = half - 2 * side
    frame = (pos // (GRID_ROWS * GRID_COLS)).astype(jnp.float32)
    row = (pos // GRID_COLS % GRID_ROWS).astype(jnp.float32)
    col = (pos % GRID_COLS).astype(jnp.float32)
    pair = jnp.arange(half, dtype=jnp.int32)
    group = jnp.where(pair < first, 0, jnp.where(pair < first + side, 1, 2))
    offset = jnp.where(group == 0, 0, jnp.where(group == 1, first, first + side))
    pairs_in = jnp.where(group == 0, first, side).astype(jnp.float32)
    freq = 10000.0 ** (-(pair - offset).astype(jnp.float32) / pairs_in)
    coord = jnp.where(group[None, :] == 0, frame[:, None], jnp.where(group[None, :] == 1, row[:, None], col[:, None]))
    angle = coord * freq[None, :]
    cosine = jnp.tile(jnp.concatenate([jnp.cos(angle), jnp.cos(angle)], axis=1), (1, HEADS))
    sine = jnp.tile(jnp.concatenate([jnp.sin(angle), jnp.sin(angle)], axis=1), (1, HEADS))
    return (cosine, sine)

def rotate(values, cosine, sine):
    count = values.shape[0]
    half = HEAD_DIM // 2
    shaped = values.reshape(count, HEADS, HEAD_DIM)
    turned = jnp.concatenate([-shaped[:, :, half:], shaped[:, :, :half]], axis=2).reshape(count, HEADS * HEAD_DIM)
    return values * cosine + turned * sine

def normalize(values, gain):
    mean_sq = lax.optimization_barrier(jnp.mean(values * values, axis=-1, keepdims=True))
    return values * lax.rsqrt(mean_sq + 1e-06) * gain

def embed(step):
    count = FREQS // 2
    freq = 10000.0 ** (-jnp.arange(count, dtype=jnp.float32) / count)
    angle = step.astype(jnp.float32) * freq
    return jnp.concatenate([jnp.cos(angle), jnp.sin(angle)])

def attention(queries, keys, values):
    count = queries.shape[0]
    qh = queries.astype(jnp.float32).reshape(count, HEADS, HEAD_DIM).transpose(1, 0, 2)
    kh = keys.astype(jnp.float32).reshape(count, HEADS, HEAD_DIM).transpose(1, 0, 2)
    vh = values.astype(jnp.float32).reshape(count, HEADS, HEAD_DIM).transpose(1, 0, 2)
    scale = 1.0 / HEAD_DIM ** 0.5

    def one_head(operands):
        qone, kone, vone = operands
        scores = jnp.dot(qone, kone.T, precision=lax.Precision.HIGHEST) * scale
        peak = lax.optimization_barrier(jnp.max(scores, axis=1, keepdims=True))
        expo = jnp.exp(scores - peak)
        total = lax.optimization_barrier(jnp.sum(expo, axis=1, keepdims=True))
        rounded = expo.astype(jnp.bfloat16).astype(jnp.float32)
        return jnp.dot(rounded, vone, precision=lax.Precision.HIGHEST) / total
    result = lax.map(one_head, (qh, kh, vh))
    return result.transpose(1, 0, 2).reshape(count, HEADS * HEAD_DIM)

def reference(qkv, qk_gain, mod_weight, positions, timesteps, cotangent):
    source = jnp.roll(qkv, 1, axis=0)
    outs = []
    grads = []
    for segment_idx in range(N_SEGMENT):
        segment_outs = []
        grad_sum = jnp.zeros((FREQS, HEADS * HEAD_DIM), jnp.float32)
        for clip_idx in range(N_DP):
            block = source[segment_idx, clip_idx].astype(jnp.float32)
            cosine, sine = rope_tables(positions[clip_idx])
            queries = rotate(normalize(block[:, 0], qk_gain[segment_idx, 0]), cosine, sine).astype(jnp.bfloat16)
            keys = rotate(normalize(block[:, 1], qk_gain[segment_idx, 1]), cosine, sine).astype(jnp.bfloat16)
            values = source[segment_idx, clip_idx, :, 2]
            attn = attention(queries, keys, values)
            emb = embed(timesteps[segment_idx, clip_idx])
            gate = jnp.dot(emb, mod_weight[segment_idx], precision=lax.Precision.HIGHEST)
            segment_outs.append((attn * gate).astype(jnp.bfloat16))
            chan = lax.optimization_barrier(jnp.sum(attn * cotangent[segment_idx, clip_idx].astype(jnp.float32), axis=0))
            grad_sum = grad_sum + emb[:, None] * chan[None, :]
        outs.append(jnp.stack(segment_outs))
        grads.append(grad_sum)
    return (jnp.stack(outs), jnp.stack(grads))
```

```python
import functools
import math

import jax
import jax.numpy as jnp
from jax import lax
from jax.experimental import pallas as pl
from jax.experimental.pallas import tpu as pltpu
from jax.sharding import PartitionSpec as P

HEAD_DIM = 128
GRID_ROWS = 45
GRID_COLS = 80
MESH = pl.DeviceIdType.MESH
LEAD = 12
LAG = 6
DIRECT = 5
BONUS = 0
TAIL = 8
FORWARD_AT = 8
VMEM_LIMIT = 24 << 20


def sincos(angle):
    turns = jnp.floor(angle * (2.0 / math.pi) + 0.5)
    quad = turns.astype(jnp.int32)
    r = angle - turns * 1.5703125
    r = r - turns * 4.837512969970703125e-4
    r = r - turns * 7.549789948768648e-8
    z = r * r
    sine = r + r * z * (-1.6666654611e-1 + z * (8.3321608736e-3 - z * 1.9515295891e-4))
    cosine = 1.0 - 0.5 * z + z * z * (
        4.166664568298827e-2 + z * (-1.388731625493765e-3 + z * 2.443315711809948e-5)
    )
    swap = (quad & 1) == 1
    s = jnp.where(swap, cosine, sine)
    c = jnp.where(swap, sine, cosine)
    s = jnp.where((quad & 2) == 2, -s, s)
    c = jnp.where(((quad + 1) & 2) == 2, -c, c)
    return s, c


def rope_angles(pos):
    count, hd = pos.shape
    half = hd // 2
    side = hd // 6
    first = half - 2 * side
    pair = lax.broadcasted_iota(jnp.int32, (8, hd), 1) % half
    group = jnp.where(pair < first, 0, jnp.where(pair < first + side, 1, 2))
    offset = jnp.where(group == 0, 0, jnp.where(group == 1, first, first + side))
    pairs_in = jnp.where(group == 0, first, side).astype(jnp.float32)
    freq = jnp.exp((pair - offset).astype(jnp.float32) / pairs_in * -math.log(10000.0))[0:1]
    group = group[0:1]
    frame = (pos // (GRID_ROWS * GRID_COLS)).astype(jnp.float32)
    row = (pos // GRID_COLS % GRID_ROWS).astype(jnp.float32)
    col = (pos % GRID_COLS).astype(jnp.float32)
    return jnp.where(group == 0, frame, jnp.where(group == 1, row, col)) * freq


def handed(seg, S):
    return DIRECT + jnp.where(seg == 0, BONUS, 0)


def body(
    S, C, D, heads, freqs,
    x_ref, gain_ref, w_ref, pos_ref, t_ref, cot_ref,
    out_ref, grad_ref,
    xv, wv, cotv, kv, qbuf, abuf, rbuf, direct, gains, posv, tbuf, gate, emb, cosv, sinv,
    part, total, late,
    load_sem, v_sem, kv_send, kv_recv, a_send, a_recv, g_send, g_recv, t_send, t_recv,
    p_send, p_recv, c_send, c_recv, l_send, l_recv,
    b_send, b_recv, bx_send, bx_recv, in_sem, down_sem, up_sem, met_sem,
):
    n = C * D
    count = x_ref.shape[1]
    rows = freqs // n
    hd = HEAD_DIM
    tail = late.shape[1]
    first = heads - tail
    seg = lax.axis_index("segment")
    ctx = lax.axis_index("ctx")
    dp = lax.axis_index("dp")
    me = ctx * D + dp
    after = {"segment": lax.rem(seg + 1, S)}
    before = {"segment": lax.rem(seg + S - 1, S)}
    early = heads - handed(seg, S)
    landed = heads - handed(before["segment"], S)
    peers = []
    for r in range(1, n):
        p = lax.rem(me + r, n)
        peers.append({"ctx": p // D, "dp": lax.rem(p, D)})
    ring = [{"ctx": lax.rem(ctx + r, C)} for r in range(1, C)]
    clips = [{"dp": lax.rem(dp + r, D)} for r in range(1, D)]

    def cols(h):
        return pl.ds(pl.multiple_of(h * hd, hd), hd)

    def tell(sem, who):
        pl.semaphore_signal(sem, inc=1, device_id=who, device_id_type=MESH)

    barrier = pltpu.get_barrier_semaphore()
    for who in ring + clips:
        tell(barrier, who)

    @pl.when(seg < S - 1)
    def _():
        tell(barrier, after)

    loads = [
        pltpu.make_async_copy(pos_ref, posv, load_sem.at[0]),
        pltpu.make_async_copy(x_ref.at[1], xv.at[1], load_sem.at[1]),
        pltpu.make_async_copy(x_ref.at[0], xv.at[0], load_sem.at[2]),
        pltpu.make_async_copy(w_ref, wv, load_sem.at[3]),
        pltpu.make_async_copy(cot_ref, cotv, load_sem.at[4]),
    ]
    for load in loads:
        load.start()

    pl.semaphore_wait(barrier, C - 1 + D - 1 + jnp.where(seg > 0, 1, 0))

    def send_values(h):
        for r in range(1, C):
            pltpu.make_async_remote_copy(
                src_ref=x_ref.at[2, :, cols(h)],
                dst_ref=kv.at[h, 1, pl.ds(r * count, count), :],
                send_sem=kv_send.at[h], recv_sem=kv_recv.at[h],
                device_id=ring[r - 1], device_id_type=MESH,
            ).start()

    def send_keys(h):
        for r in range(1, C):
            pltpu.make_async_remote_copy(
                src_ref=kv.at[h, 0, pl.ds(0, count), :],
                dst_ref=kv.at[h, 0, pl.ds(r * count, count), :],
                send_sem=kv_send.at[h], recv_sem=kv_recv.at[h],
                device_id=ring[r - 1], device_id_type=MESH,
            ).start()

    lead = min(LEAD, heads - DIRECT - BONUS)

    @pl.loop(0, lead)
    def _(h):
        send_values(h)

    for who in ring:
        tell(met_sem, who)

    gain_copy = pltpu.make_async_remote_copy(
        src_ref=gain_ref, dst_ref=gains, send_sem=g_send, recv_sem=g_recv,
        device_id=before, device_id_type=MESH,
    )

    @pl.when(seg > 0)
    def _():
        tell(in_sem, before)
        gain_copy.start()

    @pl.when(seg < S - 1)
    def _():
        pl.semaphore_wait(in_sem, 1)

    @pl.when(seg == S - 2)
    def _():
        tell(down_sem, before)

    @pl.when(seg == 1)
    def _():
        tell(up_sem, after)

    @pl.when(seg < S - 2)
    def _():
        pl.semaphore_wait(down_sem, 1)

        @pl.when(seg > 0)
        def _():
            tell(down_sem, before)

    @pl.when(seg == 0)
    def _():
        gain_copy.start()

    @pl.when(seg > 1)
    def _():
        pl.semaphore_wait(up_sem, 1)

        @pl.when(seg < S - 1)
        def _():
            tell(up_sem, after)

    def hand_over(source, which, h):
        slot = heads - 1 - h
        pltpu.make_async_remote_copy(
            src_ref=source, dst_ref=direct.at[slot, which, pl.ds(0, count), :],
            send_sem=b_send.at[slot], recv_sem=b_recv.at[slot], device_id=after, device_id_type=MESH,
        ).start()

    def own_values(h):
        return pltpu.make_async_copy(
            x_ref.at[2, :, cols(h)], kv.at[h, 1, pl.ds(0, count), :], v_sem.at[h]
        )

    @pl.loop(early, heads)
    def _(h):
        hand_over(x_ref.at[2, :, cols(h)], 1, h)

    @pl.loop(0, early)
    def _(h):
        own_values(h).start()

    loads[0].wait()
    pos = jnp.transpose(jnp.broadcast_to(posv[...], (hd, count)))
    s, c = sincos(rope_angles(pos))
    lane = lax.broadcasted_iota(jnp.int32, (count, hd), 1)
    cosv[...] = c
    sinv[...] = jnp.where(lane < hd // 2, -s, s)

    tbuf[0] = jnp.full((8, hd), t_ref[0, 0].astype(jnp.float32), jnp.float32)
    for r in range(1, D):
        pltpu.make_async_remote_copy(
            src_ref=tbuf.at[0], dst_ref=tbuf.at[r], send_sem=t_send, recv_sem=t_recv,
            device_id=clips[r - 1], device_id_type=MESH,
        ).start()

    def inverse_norm(which):
        def add(h, acc):
            x = xv[which, :, cols(h)].astype(jnp.float32)
            return acc + x * x

        acc = lax.fori_loop(0, heads, add, jnp.zeros((count, hd), jnp.float32))
        mean = jnp.sum(acc, axis=1, keepdims=True) / (heads * hd)
        return lax.rsqrt(mean + 1e-06)

    def turned(which, h, inv):
        x = xv[which, :, cols(h)].astype(jnp.float32)
        x = x * inv * gains[which : which + 1, cols(h)]
        return (x * cosv[...] + pltpu.roll(x, hd // 2, 1) * sinv[...]).astype(jnp.bfloat16)

    loads[1].wait()
    inv_k = inverse_norm(1)
    loads[2].wait()
    inv_q = inverse_norm(0)
    gain_copy.wait_recv()

    def forward(slot):
        here = direct.at[slot, :, pl.ds(0, count), :]
        pltpu.make_async_copy(here, here, b_recv.at[slot]).wait()
        for which in range(2):
            for r in range(1, C):
                pltpu.make_async_remote_copy(
                    src_ref=direct.at[slot, which, pl.ds(0, count), :],
                    dst_ref=direct.at[slot, which, pl.ds(r * count, count), :],
                    send_sem=bx_send.at[slot, which], recv_sem=bx_recv.at[slot, which],
                    device_id=ring[r - 1], device_id_type=MESH,
                ).start()

    @pl.loop(early, heads)
    def _(h):
        kv[h, 0, 0:count, :] = turned(1, h, inv_k)
        qbuf[h] = turned(0, h, inv_q)
        hand_over(kv.at[h, 0, pl.ds(0, count), :], 0, h)
        hand_over(qbuf.at[h], 2, h)

    @pl.loop(0, early)
    def _(h):
        kv[h, 0, 0:count, :] = turned(1, h, inv_k)
        send_keys(h)

        @pl.when(h + lead < early)
        def _():
            send_values(h + lead)

    @pl.loop(0, early)
    def _(h):
        qbuf[h] = turned(0, h, inv_q)

    half = freqs // 2
    decay = -math.log(10000.0) / half
    index = lax.broadcasted_iota(jnp.int32, (half, hd), 0).astype(jnp.float32)
    es, ec = sincos(tbuf[0, 0:1, :] * jnp.exp(index * decay))
    loads[3].wait()

    @pl.loop(0, heads)
    def _(h):
        terms = wv[0:half, cols(h)] * ec + wv[half:freqs, cols(h)] * es
        gate[pl.ds(h, 1), :] = jnp.sum(terms, axis=0, keepdims=True)

    if D > 1:
        others = tbuf.at[pl.ds(1, D - 1)]
        pltpu.make_async_copy(others, others, t_recv).wait()
    at = lax.broadcasted_iota(jnp.int32, (rows, hd), 0) + me * rows
    freq = jnp.exp((at % half).astype(jnp.float32) * decay)
    for j in range(D):
        s, c = sincos(tbuf[j, 0:1, :] * freq)
        emb[j] = jnp.where(at < half, c, s)
    loads[4].wait()

    scale = 1.0 / hd**0.5

    def weigh(queries, keys):
        scores = lax.dot_general(
            queries, keys, (((1,), (1,)), ((), ())), preferred_element_type=jnp.float32
        ) * scale
        expo = jnp.exp(scores - jnp.max(scores, axis=1, keepdims=True))
        return expo.astype(jnp.bfloat16), jnp.sum(expo, axis=1, keepdims=True)

    def attend(h):
        own_values(h).wait()
        arrived = kv.at[h, :, pl.ds(count, (C - 1) * count), :]
        pltpu.make_async_copy(arrived, arrived, kv_recv.at[h]).wait()
        weights, norm = weigh(qbuf[h], kv[h, 0])
        mixed = jnp.dot(weights, kv[h, 1], preferred_element_type=jnp.float32)
        abuf[h] = (mixed / norm).astype(jnp.bfloat16)
        pltpu.make_async_remote_copy(
            src_ref=abuf.at[h], dst_ref=rbuf.at[h], send_sem=a_send.at[h], recv_sem=a_recv.at[h],
            device_id=after, device_id_type=MESH,
        ).start()

    def use(h, attn):
        out_ref[:, cols(h)] = (attn * gate[pl.ds(h, 1), :]).astype(jnp.bfloat16)
        cot = cotv[:, cols(h)].astype(jnp.float32)
        return jnp.sum(attn * cot, axis=0, keepdims=True)

    def finish(h):
        pltpu.make_async_copy(rbuf.at[h], rbuf.at[h], a_recv.at[h]).wait()
        return use(h, rbuf[h].astype(jnp.float32))

    @pl.loop(0, early)
    def _(h):
        attend(h)

        @pl.when(h == FORWARD_AT)
        def _():
            @pl.loop(landed, heads - 1)
            def _(g):
                forward(heads - 1 - g)

        @pl.when(h >= LAG)
        def _():
            part[0, pl.ds(h - LAG, 1), :] = finish(h - LAG)

    @pl.loop(early - LAG, first)
    def _(h):
        part[0, pl.ds(h, 1), :] = finish(h)

    for r in range(1, C):
        pltpu.make_async_remote_copy(
            src_ref=part.at[0], dst_ref=part.at[r], send_sem=p_send, recv_sem=p_recv,
            device_id=ring[r - 1], device_id_type=MESH,
        ).start()
    forward(0)

    @pl.loop(first, landed)
    def _(h):
        late[0, pl.ds(h - first, 1), :] = finish(h)

    def direct_head(h):
        slot = heads - 1 - h
        arrived = direct.at[slot, 0, pl.ds(count, (C - 1) * count), :]
        pltpu.make_async_copy(arrived, arrived, bx_recv.at[slot, 0]).wait()
        weights, norm = weigh(direct[slot, 2, 0:count, :], direct[slot, 0])
        arrived = direct.at[slot, 1, pl.ds(count, (C - 1) * count), :]
        pltpu.make_async_copy(arrived, arrived, bx_recv.at[slot, 1]).wait()
        mixed = jnp.dot(weights, direct[slot, 1], preferred_element_type=jnp.float32)
        late[0, pl.ds(h - first, 1), :] = use(h, mixed / norm)

    @pl.loop(landed, heads - 1)
    def _(h):
        direct_head(h)

    if C > 1:
        others = part.at[pl.ds(1, C - 1)]
        pltpu.make_async_copy(others, others, p_recv).wait()
    acc = part[0]
    for r in range(1, C):
        acc = acc + part[r]
    total[0] = acc
    for r in range(1, D):
        pltpu.make_async_remote_copy(
            src_ref=total.at[0], dst_ref=total.at[r], send_sem=c_send, recv_sem=c_recv,
            device_id=clips[r - 1], device_id_type=MESH,
        ).start()
    pl.semaphore_wait(met_sem, C - 1)

    direct_head(heads - 1)
    order = sorted(range(1, n), key=lambda r: (r % D == 0) + (r < D or r > n - D))
    for r in order:
        pltpu.make_async_remote_copy(
            src_ref=late.at[0], dst_ref=late.at[r], send_sem=l_send, recv_sem=l_recv,
            device_id=peers[r - 1], device_id_type=MESH,
        ).start()

    gain_copy.wait_send()
    if D > 1:
        others = tbuf.at[pl.ds(1, D - 1)]
        pltpu.make_async_copy(others, others, t_send).wait()
        others = total.at[pl.ds(1, D - 1)]
        pltpu.make_async_copy(others, others, c_recv).wait()
        pltpu.make_async_copy(others, others, c_send).wait()
    if C > 1:
        others = part.at[pl.ds(1, C - 1)]
        pltpu.make_async_copy(others, others, p_send).wait()

    @pl.loop(0, first)
    def _(h):
        acc = emb[0] * total[0, pl.ds(h, 1), :]
        for j in range(1, D):
            acc = acc + emb[j] * total[j, pl.ds(h, 1), :]
        grad_ref[:, cols(h)] = acc

    @pl.loop(0, early)
    def _(h):
        sent = kv.at[h, :, pl.ds(count, (C - 1) * count), :]
        pltpu.make_async_copy(sent, sent, kv_send.at[h]).wait()
        pltpu.make_async_copy(abuf.at[h], abuf.at[h], a_send.at[h]).wait()

    @pl.loop(early, heads)
    def _(h):
        given = direct.at[heads - 1 - h, :, pl.ds(0, count), :]
        pltpu.make_async_copy(given, given, b_send.at[heads - 1 - h]).wait()

    @pl.loop(landed, heads)
    def _(h):
        for which in range(2):
            sent = direct.at[heads - 1 - h, which, pl.ds(count, (C - 1) * count), :]
            pltpu.make_async_copy(sent, sent, bx_send.at[heads - 1 - h, which]).wait()

    if n > 1:
        others = late.at[pl.ds(1, n - 1)]
        pltpu.make_async_copy(others, others, l_recv).wait()
        pltpu.make_async_copy(others, others, l_send).wait()

    sums = []
    for j in range(D):
        acc = late[j]
        for c in range(1, C):
            acc = acc + late[j + c * D]
        sums.append(acc)
    for i in range(tail):
        acc = emb[0] * sums[0][i : i + 1, :]
        for j in range(1, D):
            acc = acc + emb[j] * sums[j][i : i + 1, :]
        grad_ref[:, (first + i) * hd : (first + i + 1) * hd] = acc


def store(attn_ref, grad_ref, out_ref, grads_ref, out_sem, grad_sem):
    copies = [
        pltpu.make_async_copy(attn_ref, out_ref, out_sem),
        pltpu.make_async_copy(grad_ref, grads_ref, grad_sem),
    ]
    for copy in copies:
        copy.start()
    for copy in copies:
        copy.wait()


def local(S, C, D, qkv, qk_gain, mod_weight, positions, timesteps, cotangent):
    count, _, width = qkv.shape[2:]
    freqs = mod_weight.shape[1]
    heads = width // HEAD_DIM
    n = C * D
    rows = freqs // n
    hd = HEAD_DIM
    tail = min(TAIL, heads - 1)
    most = DIRECT + BONUS
    if S < 3 or n < 2 or tail < most or heads - most - LAG < 1:
        raise ValueError("unsupported mesh")
    bf, f32 = jnp.bfloat16, jnp.float32
    vmem = pl.BlockSpec(memory_space=pltpu.VMEM)
    hbm = pl.BlockSpec(memory_space=pltpu.HBM)
    dma = pltpu.SemaphoreType.DMA
    regular = pltpu.SemaphoreType.REGULAR
    pin = functools.partial(pltpu.with_memory_space_constraint, memory_space=pltpu.HBM)
    attn, grad = pl.pallas_call(
        functools.partial(body, S, C, D, heads, freqs),
        out_shape=(
            jax.ShapeDtypeStruct((count, width), bf),
            jax.ShapeDtypeStruct((rows, width), f32),
        ),
        in_specs=[hbm] * 4 + [pl.BlockSpec(memory_space=pltpu.SMEM), hbm],
        out_specs=(vmem, vmem),
        scratch_shapes=[
            pltpu.VMEM((2, count, width), bf),
            pltpu.VMEM((freqs, width), f32),
            pltpu.VMEM((count, width), bf),
            pltpu.VMEM((heads, 2, C * count, hd), bf),
            pltpu.VMEM((heads, count, hd), bf),
            pltpu.VMEM((heads, count, hd), bf),
            pltpu.VMEM((heads, count, hd), bf),
            pltpu.VMEM((most, 3, C * count, hd), bf),
            pltpu.VMEM((2, width), f32),
            pltpu.VMEM((1, count), jnp.int32),
            pltpu.VMEM((D, 8, hd), f32),
            pltpu.VMEM((-(-heads // 8) * 8, hd), f32),
            pltpu.VMEM((D, rows, hd), f32),
            pltpu.VMEM((count, hd), f32),
            pltpu.VMEM((count, hd), f32),
            pltpu.VMEM((C, heads - tail, hd), f32),
            pltpu.VMEM((D, heads - tail, hd), f32),
            pltpu.VMEM((n, tail, hd), f32),
            dma((5,)), dma((heads,)),
            dma((heads,)), dma((heads,)), dma((heads,)), dma((heads,)),
            dma, dma, dma, dma, dma, dma, dma, dma, dma, dma,
            dma((most,)), dma((most,)), dma((most, 2)), dma((most, 2)),
            regular, regular, regular, regular,
        ],
        compiler_params=pltpu.CompilerParams(
            collective_id=0, has_side_effects=True, vmem_limit_bytes=VMEM_LIMIT if C <= 2 else 60 << 20
        ),
    )(
        pin(jnp.moveaxis(qkv[0, 0], 1, 0)),
        pin(qk_gain[0]),
        pin(mod_weight[0]),
        pin(positions),
        timesteps,
        pin(cotangent[0, 0]),
    )
    anywhere = pl.BlockSpec(memory_space=pl.ANY)
    attn_out, gate_grad = pl.pallas_call(
        store,
        out_shape=(
            jax.ShapeDtypeStruct((count, width), bf),
            jax.ShapeDtypeStruct((rows, width), f32),
        ),
        in_specs=[anywhere, anywhere],
        out_specs=(anywhere, anywhere),
        scratch_shapes=[dma, dma],
        compiler_params=pltpu.CompilerParams(vmem_limit_bytes=4 << 20),
    )(attn, grad)
    return attn_out[None, None], gate_grad[None]


def solution(mesh):
    sizes = mesh.shape
    return jax.shard_map(
        functools.partial(local, sizes["segment"], sizes["ctx"], sizes["dp"]),
        mesh=mesh,
        in_specs=(
            P("segment", "dp", "ctx", None, None),
            P("segment", None, None),
            P("segment", None, None),
            P("dp", "ctx"),
            P("segment", "dp"),
            P("segment", "dp", "ctx", None),
        ),
        out_specs=(P("segment", "dp", "ctx", None), P("segment", ("ctx", "dp"), None)),
        check_vma=False,
    )
```

```python
import functools
import math

import jax
import jax.numpy as jnp
from jax import lax
from jax.experimental import pallas as pl
from jax.experimental.pallas import tpu as pltpu
from jax.sharding import PartitionSpec as P

HEAD_DIM = 128
GRID_ROWS = 45
GRID_COLS = 80
MESH = pl.DeviceIdType.MESH
LEAD = 12
GROUP = 3
LAG = 3
DIRECT = 5
FIRST = 9
FORWARD_AT = 8
VMEM_LIMIT = 24 << 20


def sincos(angle):
    turns = jnp.floor(angle * (2.0 / math.pi) + 0.5)
    quad = turns.astype(jnp.int32)
    r = angle - turns * 1.5703125
    r = r - turns * 4.837512969970703125e-4
    r = r - turns * 7.549789948768648e-8
    z = r * r
    sine = r + r * z * (-1.6666654611e-1 + z * (8.3321608736e-3 - z * 1.9515295891e-4))
    cosine = 1.0 - 0.5 * z + z * z * (
        4.166664568298827e-2 + z * (-1.388731625493765e-3 + z * 2.443315711809948e-5)
    )
    swap = (quad & 1) == 1
    s = jnp.where(swap, cosine, sine)
    c = jnp.where(swap, sine, cosine)
    s = jnp.where((quad & 2) == 2, -s, s)
    c = jnp.where(((quad + 1) & 2) == 2, -c, c)
    return s, c


def rope_angles(pos):
    count, hd = pos.shape
    half = hd // 2
    side = hd // 6
    first = half - 2 * side
    pair = lax.broadcasted_iota(jnp.int32, (8, hd), 1) % half
    group = jnp.where(pair < first, 0, jnp.where(pair < first + side, 1, 2))
    offset = jnp.where(group == 0, 0, jnp.where(group == 1, first, first + side))
    pairs_in = jnp.where(group == 0, first, side).astype(jnp.float32)
    freq = jnp.exp((pair - offset).astype(jnp.float32) / pairs_in * -math.log(10000.0))[0:1]
    group = group[0:1]
    frame = (pos // (GRID_ROWS * GRID_COLS)).astype(jnp.float32)
    row = (pos // GRID_COLS % GRID_ROWS).astype(jnp.float32)
    col = (pos % GRID_COLS).astype(jnp.float32)
    return jnp.where(group == 0, frame, jnp.where(group == 1, row, col)) * freq


def body(
    S, C, D, heads, freqs,
    x_ref, gain_ref, w_ref, pos_ref, t_ref, cot_ref,
    out_ref, grad_ref,
    xv, wv, cotv, kv, qbuf, abuf, rbuf, direct, gains, posv, tbuf, gate, emb, cosv, sinv,
    part, total, late, last,
    load_sem, v_sem, kv_send, kv_recv, a_send, a_recv, g_send, g_recv, t_send, t_recv,
    p_send, p_recv, c_send, c_recv, l_send, l_recv, m_send, m_recv,
    b_send, b_recv, bx_send, bx_recv, in_sem, down_sem, up_sem, met_sem, dp_sem,
):
    n = C * D
    count = x_ref.shape[1]
    rows = freqs // n
    hd = HEAD_DIM
    first = part.shape[1]
    seg = lax.axis_index("segment")
    ctx = lax.axis_index("ctx")
    dp = lax.axis_index("dp")
    me = ctx * D + dp
    after = {"segment": lax.rem(seg + 1, S)}
    before = {"segment": lax.rem(seg + S - 1, S)}
    early = heads - direct.shape[0]
    peers = []
    for r in range(1, n):
        p = lax.rem(me + r, n)
        peers.append({"ctx": p // D, "dp": lax.rem(p, D)})
    ring = [{"ctx": lax.rem(ctx + r, C)} for r in range(1, C)]
    clips = [{"dp": lax.rem(dp + r, D)} for r in range(1, D)]

    def cols(h):
        return pl.ds(pl.multiple_of(h * hd, hd), hd)

    def tell(sem, who):
        pl.semaphore_signal(sem, inc=1, device_id=who, device_id_type=MESH)

    barrier = pltpu.get_barrier_semaphore()
    for who in ring:
        tell(barrier, who)

    @pl.loop(dp + 1, D)
    def _(d):
        tell(barrier, {"dp": d})

    @pl.when(seg < S - 1)
    def _():
        tell(barrier, after)

    loads = [
        pltpu.make_async_copy(pos_ref, posv, load_sem.at[0]),
        pltpu.make_async_copy(x_ref.at[1], xv.at[1], load_sem.at[1]),
        pltpu.make_async_copy(x_ref.at[0], xv.at[0], load_sem.at[2]),
        pltpu.make_async_copy(w_ref, wv, load_sem.at[3]),
        pltpu.make_async_copy(cot_ref, cotv, load_sem.at[4]),
    ]
    for load in loads[:3]:
        load.start()

    pl.semaphore_wait(barrier, C - 1 + dp + jnp.where(seg > 0, 1, 0))

    def send_values(h):
        for r in range(1, C):
            pltpu.make_async_remote_copy(
                src_ref=x_ref.at[2, :, cols(h)],
                dst_ref=kv.at[h, 1, pl.ds(r * count, count), :],
                send_sem=kv_send, recv_sem=kv_recv.at[h],
                device_id=ring[r - 1], device_id_type=MESH,
            ).start()

    def send_keys(h):
        for r in range(1, C):
            pltpu.make_async_remote_copy(
                src_ref=kv.at[h, 0, pl.ds(0, count), :],
                dst_ref=kv.at[h, 0, pl.ds(r * count, count), :],
                send_sem=kv_send, recv_sem=kv_recv.at[h],
                device_id=ring[r - 1], device_id_type=MESH,
            ).start()

    lead = min(LEAD, early)

    @pl.loop(0, lead)
    def _(h):
        send_values(h)

    @pl.loop(0, dp)
    def _(d):
        tell(dp_sem, {"dp": d})

    @pl.loop(0, heads)
    def _(h):
        pltpu.make_async_copy(x_ref.at[2, :, cols(h)], kv.at[h, 1, pl.ds(0, count), :], v_sem).start()

    for load in loads[3:]:
        load.start()

    gain_copy = pltpu.make_async_remote_copy(
        src_ref=gain_ref, dst_ref=gains, send_sem=g_send, recv_sem=g_recv,
        device_id=before, device_id_type=MESH,
    )

    @pl.when(seg > 0)
    def _():
        tell(in_sem, before)
        gain_copy.start()

    @pl.when(seg < S - 1)
    def _():
        pl.semaphore_wait(in_sem, 1)

    @pl.when(seg == S - 2)
    def _():
        tell(down_sem, before)

    @pl.when(seg == 1)
    def _():
        tell(up_sem, after)

    @pl.when(seg < S - 2)
    def _():
        pl.semaphore_wait(down_sem, 1)

        @pl.when(seg > 0)
        def _():
            tell(down_sem, before)

    @pl.when(seg == 0)
    def _():
        gain_copy.start()

    @pl.when(seg > 1)
    def _():
        pl.semaphore_wait(up_sem, 1)

        @pl.when(seg < S - 1)
        def _():
            tell(up_sem, after)

    @pl.when(dp < D - 1)
    def _():
        pl.semaphore_wait(dp_sem, D - 1 - dp)

    for who in ring:
        tell(met_sem, who)
    own = kv.at[:, 1, pl.ds(0, count), :]
    pltpu.make_async_copy(own, own, v_sem).wait()

    def hand_over(source, which, h):
        slot = heads - 1 - h
        pltpu.make_async_remote_copy(
            src_ref=source, dst_ref=direct.at[slot, which, pl.ds(0, count), :],
            send_sem=b_send, recv_sem=b_recv, device_id=after, device_id_type=MESH,
        ).start()

    @pl.loop(early, heads)
    def _(h):
        hand_over(kv.at[h, 1, pl.ds(0, count), :], 1, h)

    loads[0].wait()
    pos = jnp.transpose(jnp.broadcast_to(posv[...], (hd, count)))
    s, c = sincos(rope_angles(pos))
    lane = lax.broadcasted_iota(jnp.int32, (count, hd), 1)
    cosv[...] = c
    sinv[...] = jnp.where(lane < hd // 2, -s, s)

    tbuf[0] = jnp.full((8, hd), t_ref[0, 0].astype(jnp.float32), jnp.float32)
    for r in range(1, D):
        pltpu.make_async_remote_copy(
            src_ref=tbuf.at[0], dst_ref=tbuf.at[r], send_sem=t_send, recv_sem=t_recv,
            device_id=clips[r - 1], device_id_type=MESH,
        ).start()

    def inverse_norm(which):
        def add(h, acc):
            x = xv[which, :, cols(h)].astype(jnp.float32)
            return acc + x * x

        acc = lax.fori_loop(0, heads, add, jnp.zeros((count, hd), jnp.float32))
        mean = jnp.sum(acc, axis=1, keepdims=True) / (heads * hd)
        return lax.rsqrt(mean + 1e-06)

    def turned(which, h, inv):
        x = xv[which, :, cols(h)].astype(jnp.float32)
        x = x * inv * gains[which : which + 1, cols(h)]
        return (x * cosv[...] + pltpu.roll(x, hd // 2, 1) * sinv[...]).astype(jnp.bfloat16)

    loads[1].wait()
    inv_k = inverse_norm(1)
    loads[2].wait()
    inv_q = inverse_norm(0)
    gain_copy.wait_recv()

    def forward(slot):
        for which in range(2):
            for r in range(1, C):
                pltpu.make_async_remote_copy(
                    src_ref=direct.at[slot, which, pl.ds(0, count), :],
                    dst_ref=direct.at[slot, which, pl.ds(r * count, count), :],
                    send_sem=bx_send, recv_sem=bx_recv.at[slot * 2 + which],
                    device_id=ring[r - 1], device_id_type=MESH,
                ).start()

    @pl.loop(0, early)
    def _(h):
        kv[h, 0, 0:count, :] = turned(1, h, inv_k)
        send_keys(h)

        @pl.when(h + lead < early)
        def _():
            send_values(h + lead)

    @pl.loop(early, heads)
    def _(h):
        kv[h, 0, 0:count, :] = turned(1, h, inv_k)
        qbuf[h] = turned(0, h, inv_q)
        hand_over(kv.at[h, 0, pl.ds(0, count), :], 0, h)
        hand_over(qbuf.at[h], 2, h)

    @pl.loop(0, early)
    def _(h):
        qbuf[h] = turned(0, h, inv_q)

    half = freqs // 2
    decay = -math.log(10000.0) / half
    index = lax.broadcasted_iota(jnp.int32, (half, hd), 0).astype(jnp.float32)
    es, ec = sincos(tbuf[0, 0:1, :] * jnp.exp(index * decay))
    loads[3].wait()

    @pl.loop(0, heads)
    def _(h):
        terms = wv[0:half, cols(h)] * ec + wv[half:freqs, cols(h)] * es
        gate[pl.ds(h, 1), :] = jnp.sum(terms, axis=0, keepdims=True)

    if D > 1:
        others = tbuf.at[pl.ds(1, D - 1)]
        pltpu.make_async_copy(others, others, t_recv).wait()
    at = lax.broadcasted_iota(jnp.int32, (rows, hd), 0) + me * rows
    freq = jnp.exp((at % half).astype(jnp.float32) * decay)
    for j in range(D):
        s, c = sincos(tbuf[j, 0:1, :] * freq)
        emb[j] = jnp.where(at < half, c, s)
    loads[4].wait()

    scale = 1.0 / hd**0.5

    def weigh(queries, keys):
        scores = lax.dot_general(
            queries, keys, (((1,), (1,)), ((), ())), preferred_element_type=jnp.float32
        ) * scale
        expo = jnp.exp(scores - jnp.max(scores, axis=1, keepdims=True))
        return expo.astype(jnp.bfloat16), jnp.sum(expo, axis=1, keepdims=True)

    def attend(h):
        arrived = kv.at[h, :, pl.ds(count, (C - 1) * count), :]
        pltpu.make_async_copy(arrived, arrived, kv_recv.at[h]).wait()
        weights, norm = weigh(qbuf[h], kv[h, 0])
        mixed = jnp.dot(weights, kv[h, 1], preferred_element_type=jnp.float32)
        abuf[h] = (mixed / norm).astype(jnp.bfloat16)
        pltpu.make_async_remote_copy(
            src_ref=abuf.at[h], dst_ref=rbuf.at[h], send_sem=a_send, recv_sem=a_recv.at[h // GROUP],
            device_id=after, device_id_type=MESH,
        ).start()

    def use(h, attn):
        out_ref[:, cols(h)] = (attn * gate[pl.ds(h, 1), :]).astype(jnp.bfloat16)
        cot = cotv[:, cols(h)].astype(jnp.float32)
        return jnp.sum(attn * cot, axis=0, keepdims=True)

    def finish(g):
        some = rbuf.at[pl.ds(g * GROUP, GROUP)]
        pltpu.make_async_copy(some, some, a_recv.at[g]).wait()
        for i in range(GROUP):
            h = g * GROUP + i
            part[0, pl.ds(h, 1), :] = use(h, rbuf[h].astype(jnp.float32))

    @pl.loop(0, early)
    def _(h):
        attend(h)

        @pl.when(h == FORWARD_AT)
        def _():
            here = direct.at[:, :, pl.ds(0, count), :]
            pltpu.make_async_copy(here, here, b_recv).wait()

            @pl.loop(early, heads - 1)
            def _(g):
                forward(heads - 1 - g)

        @pl.when(jnp.logical_and(lax.rem(h, GROUP) == GROUP - 1, h >= LAG * GROUP))
        def _():
            finish(h // GROUP - LAG)

    groups = early // GROUP

    @pl.loop(max(groups - LAG, 0), first // GROUP)
    def _(g):
        finish(g)

    for r in range(1, C):
        pltpu.make_async_remote_copy(
            src_ref=part.at[0], dst_ref=part.at[r], send_sem=p_send, recv_sem=p_recv,
            device_id=ring[r - 1], device_id_type=MESH,
        ).start()

    def direct_head(h):
        slot = heads - 1 - h
        for which in range(2):
            arrived = direct.at[slot, which, pl.ds(count, (C - 1) * count), :]
            pltpu.make_async_copy(arrived, arrived, bx_recv.at[slot * 2 + which]).wait()
            if which == 0:
                weights, norm = weigh(direct[slot, 2, 0:count, :], direct[slot, 0])
        mixed = jnp.dot(weights, direct[slot, 1], preferred_element_type=jnp.float32)
        return use(h, mixed / norm)

    forward(0)

    @pl.loop(early, heads - 1)
    def _(h):
        late[0, pl.ds(h - first, 1), :] = direct_head(h)

    @pl.loop(first // GROUP, groups)
    def _(g):
        some = rbuf.at[pl.ds(g * GROUP, GROUP)]
        pltpu.make_async_copy(some, some, a_recv.at[g]).wait()
        for i in range(GROUP):
            h = g * GROUP + i
            late[0, pl.ds(h - first, 1), :] = use(h, rbuf[h].astype(jnp.float32))

    pl.semaphore_wait(met_sem, C - 1)
    order = sorted(range(1, n), key=lambda r: (r % D == 0) + (r < D or r > n - D))

    def share(rows_of, send, recv):
        for r in order:
            pltpu.make_async_remote_copy(
                src_ref=rows_of.at[0], dst_ref=rows_of.at[r], send_sem=send, recv_sem=recv,
                device_id=peers[r - 1], device_id_type=MESH,
            ).start()

    share(late, l_send, l_recv)
    last[0] = direct_head(heads - 1)
    share(last, m_send, m_recv)

    if C > 1:
        others = part.at[pl.ds(1, C - 1)]
        pltpu.make_async_copy(others, others, p_recv).wait()
    acc = part[0]
    for r in range(1, C):
        acc = acc + part[r]
    total[0] = acc
    for r in range(1, D):
        pltpu.make_async_remote_copy(
            src_ref=total.at[0], dst_ref=total.at[r], send_sem=c_send, recv_sem=c_recv,
            device_id=clips[r - 1], device_id_type=MESH,
        ).start()

    gain_copy.wait_send()
    if D > 1:
        others = tbuf.at[pl.ds(1, D - 1)]
        pltpu.make_async_copy(others, others, t_send).wait()
        others = total.at[pl.ds(1, D - 1)]
        pltpu.make_async_copy(others, others, c_recv).wait()
        pltpu.make_async_copy(others, others, c_send).wait()
    if C > 1:
        others = part.at[pl.ds(1, C - 1)]
        pltpu.make_async_copy(others, others, p_send).wait()

    @pl.loop(0, first)
    def _(h):
        acc = emb[0] * total[0, pl.ds(h, 1), :]
        for j in range(1, D):
            acc = acc + emb[j] * total[j, pl.ds(h, 1), :]
        grad_ref[:, cols(h)] = acc

    sent = kv.at[pl.ds(0, early), :, pl.ds(count, (C - 1) * count), :]
    pltpu.make_async_copy(sent, sent, kv_send).wait()
    sent = abuf.at[pl.ds(0, early)]
    pltpu.make_async_copy(sent, sent, a_send).wait()
    sent = direct.at[:, :, pl.ds(0, count), :]
    pltpu.make_async_copy(sent, sent, b_send).wait()
    sent = direct.at[:, pl.ds(0, 2), pl.ds(count, (C - 1) * count), :]
    pltpu.make_async_copy(sent, sent, bx_send).wait()

    def grads(rows_of, recv, send, start):
        others = rows_of.at[pl.ds(1, n - 1)]
        pltpu.make_async_copy(others, others, recv).wait()
        sums = []
        for j in range(D):
            acc = rows_of[j]
            for c in range(1, C):
                acc = acc + rows_of[j + c * D]
            sums.append(acc)
        for i in range(rows_of.shape[1]):
            acc = emb[0] * sums[0][i : i + 1, :]
            for j in range(1, D):
                acc = acc + emb[j] * sums[j][i : i + 1, :]
            grad_ref[:, (start + i) * hd : (start + i + 1) * hd] = acc
        pltpu.make_async_copy(others, others, send).wait()

    grads(late, l_recv, l_send, first)
    grads(last, m_recv, m_send, heads - 1)


def store(attn_ref, grad_ref, out_ref, grads_ref, out_sem, grad_sem):
    copies = [
        pltpu.make_async_copy(attn_ref, out_ref, out_sem),
        pltpu.make_async_copy(grad_ref, grads_ref, grad_sem),
    ]
    for copy in copies:
        copy.start()
    for copy in copies:
        copy.wait()


def local(S, C, D, qkv, qk_gain, mod_weight, positions, timesteps, cotangent):
    count, _, width = qkv.shape[2:]
    freqs = mod_weight.shape[1]
    heads = width // HEAD_DIM
    n = C * D
    rows = freqs // n
    hd = HEAD_DIM
    most = DIRECT
    early = heads - most
    first = FIRST
    if S < 3 or n < 2 or early % GROUP or first % GROUP or first > early or FORWARD_AT >= early:
        raise ValueError("unsupported mesh")
    bf, f32 = jnp.bfloat16, jnp.float32
    vmem = pl.BlockSpec(memory_space=pltpu.VMEM)
    hbm = pl.BlockSpec(memory_space=pltpu.HBM)
    dma = pltpu.SemaphoreType.DMA
    regular = pltpu.SemaphoreType.REGULAR
    pin = functools.partial(pltpu.with_memory_space_constraint, memory_space=pltpu.HBM)
    attn, grad = pl.pallas_call(
        functools.partial(body, S, C, D, heads, freqs),
        out_shape=(
            jax.ShapeDtypeStruct((count, width), bf),
            jax.ShapeDtypeStruct((rows, width), f32),
        ),
        in_specs=[hbm] * 4 + [pl.BlockSpec(memory_space=pltpu.SMEM), hbm],
        out_specs=(vmem, vmem),
        scratch_shapes=[
            pltpu.VMEM((2, count, width), bf),
            pltpu.VMEM((freqs, width), f32),
            pltpu.VMEM((count, width), bf),
            pltpu.VMEM((heads, 2, C * count, hd), bf),
            pltpu.VMEM((heads, count, hd), bf),
            pltpu.VMEM((heads, count, hd), bf),
            pltpu.VMEM((heads, count, hd), bf),
            pltpu.VMEM((most, 3, C * count, hd), bf),
            pltpu.VMEM((2, width), f32),
            pltpu.VMEM((1, count), jnp.int32),
            pltpu.VMEM((D, 8, hd), f32),
            pltpu.VMEM((-(-heads // 8) * 8, hd), f32),
            pltpu.VMEM((D, rows, hd), f32),
            pltpu.VMEM((count, hd), f32),
            pltpu.VMEM((count, hd), f32),
            pltpu.VMEM((C, first, hd), f32),
            pltpu.VMEM((D, first, hd), f32),
            pltpu.VMEM((n, heads - 1 - first, hd), f32),
            pltpu.VMEM((n, 1, hd), f32),
            dma((5,)), dma,
            dma, dma((early,)), dma, dma((early // GROUP,)),
            dma, dma, dma, dma, dma, dma, dma, dma, dma, dma, dma, dma,
            dma, dma, dma, dma((most * 2,)),
            regular, regular, regular, regular, regular,
        ],
        compiler_params=pltpu.CompilerParams(
            collective_id=0, has_side_effects=True, vmem_limit_bytes=VMEM_LIMIT if C <= 2 else 60 << 20
        ),
    )(
        pin(jnp.moveaxis(qkv[0, 0], 1, 0)),
        pin(qk_gain[0]),
        pin(mod_weight[0]),
        pin(positions),
        timesteps,
        pin(cotangent[0, 0]),
    )
    anywhere = pl.BlockSpec(memory_space=pl.ANY)
    attn_out, gate_grad = pl.pallas_call(
        store,
        out_shape=(
            jax.ShapeDtypeStruct((count, width), bf),
            jax.ShapeDtypeStruct((rows, width), f32),
        ),
        in_specs=[anywhere, anywhere],
        out_specs=(anywhere, anywhere),
        scratch_shapes=[dma, dma],
        compiler_params=pltpu.CompilerParams(vmem_limit_bytes=4 << 20),
    )(attn, grad)
    return attn_out[None, None], gate_grad[None]


def solution(mesh):
    sizes = mesh.shape
    return jax.shard_map(
        functools.partial(local, sizes["segment"], sizes["ctx"], sizes["dp"]),
        mesh=mesh,
        in_specs=(
            P("segment", "dp", "ctx", None, None),
            P("segment", None, None),
            P("segment", None, None),
            P("dp", "ctx"),
            P("segment", "dp"),
            P("segment", "dp", "ctx", None),
        ),
        out_specs=(P("segment", "dp", "ctx", None), P("segment", ("ctx", "dp"), None)),
        check_vma=False,
    )
```

```python
import functools
import math

import jax
import jax.numpy as jnp
from jax import lax
from jax.experimental import pallas as pl
from jax.experimental.pallas import tpu as pltpu
from jax.sharding import PartitionSpec as P

HEAD_DIM = 128
GRID_ROWS = 45
GRID_COLS = 80
MESH = pl.DeviceIdType.MESH
LEAD = 12
GROUP = 3
LAG = 3
DIRECT = 5
FIRST = 9
GIVER = 0
FORWARD_AT = 8
VMEM_LIMIT = 24 << 20


def sincos(angle):
    turns = jnp.floor(angle * (2.0 / math.pi) + 0.5)
    quad = turns.astype(jnp.int32)
    r = angle - turns * 1.5703125
    r = r - turns * 4.837512969970703125e-4
    r = r - turns * 7.549789948768648e-8
    z = r * r
    sine = r + r * z * (-1.6666654611e-1 + z * (8.3321608736e-3 - z * 1.9515295891e-4))
    cosine = 1.0 - 0.5 * z + z * z * (
        4.166664568298827e-2 + z * (-1.388731625493765e-3 + z * 2.443315711809948e-5)
    )
    swap = (quad & 1) == 1
    s = jnp.where(swap, cosine, sine)
    c = jnp.where(swap, sine, cosine)
    s = jnp.where((quad & 2) == 2, -s, s)
    c = jnp.where(((quad + 1) & 2) == 2, -c, c)
    return s, c


def rope_angles(pos):
    count, hd = pos.shape
    half = hd // 2
    side = hd // 6
    first = half - 2 * side
    pair = lax.broadcasted_iota(jnp.int32, (8, hd), 1) % half
    group = jnp.where(pair < first, 0, jnp.where(pair < first + side, 1, 2))
    offset = jnp.where(group == 0, 0, jnp.where(group == 1, first, first + side))
    pairs_in = jnp.where(group == 0, first, side).astype(jnp.float32)
    freq = jnp.exp((pair - offset).astype(jnp.float32) / pairs_in * -math.log(10000.0))[0:1]
    group = group[0:1]
    frame = (pos // (GRID_ROWS * GRID_COLS)).astype(jnp.float32)
    row = (pos // GRID_COLS % GRID_ROWS).astype(jnp.float32)
    col = (pos % GRID_COLS).astype(jnp.float32)
    return jnp.where(group == 0, frame, jnp.where(group == 1, row, col)) * freq


def body(
    S, C, D, heads, freqs,
    x_ref, gain_ref, w_ref, pos_ref, t_ref, cot_ref,
    out_ref, grad_ref,
    xv, wv, cotv, kv, qbuf, abuf, rbuf, direct, gains, posv, tbuf, gate, emb, cosv, sinv,
    part, total, late, last,
    load_sem, v_sem, kv_send, kv_recv, a_send, a_recv, g_send, g_recv, t_send, t_recv,
    p_send, p_recv, c_send, c_recv, l_send, l_recv, m_send, m_recv,
    b_send, b_recv, bx_send, bx_recv, e_send, e_recv, ex_send, ex_recv, in_sem, down_sem, up_sem, met_sem, dp_sem,
):
    n = C * D
    count = x_ref.shape[1]
    rows = freqs // n
    hd = HEAD_DIM
    first = part.shape[1]
    seg = lax.axis_index("segment")
    ctx = lax.axis_index("ctx")
    dp = lax.axis_index("dp")
    me = ctx * D + dp
    after = {"segment": lax.rem(seg + 1, S)}
    before = {"segment": lax.rem(seg + S - 1, S)}
    most = direct.shape[0] - 1
    early = heads - most
    edge = dp == D - 1
    give = jnp.logical_and(seg == GIVER, edge)
    take = jnp.logical_and(seg == GIVER + 1, edge)
    mine = early - jnp.where(give, 1, 0)
    peers = []
    for r in range(1, n):
        p = lax.rem(me + r, n)
        peers.append({"ctx": p // D, "dp": lax.rem(p, D)})
    ring = [{"ctx": lax.rem(ctx + r, C)} for r in range(1, C)]
    clips = [{"dp": lax.rem(dp + r, D)} for r in range(1, D)]

    def cols(h):
        return pl.ds(pl.multiple_of(h * hd, hd), hd)

    def tell(sem, who):
        pl.semaphore_signal(sem, inc=1, device_id=who, device_id_type=MESH)

    barrier = pltpu.get_barrier_semaphore()
    for who in ring:
        tell(barrier, who)

    @pl.loop(dp + 1, D)
    def _(d):
        tell(barrier, {"dp": d})

    @pl.when(seg < S - 1)
    def _():
        tell(barrier, after)

    loads = [
        pltpu.make_async_copy(pos_ref, posv, load_sem.at[0]),
        pltpu.make_async_copy(x_ref.at[1], xv.at[1], load_sem.at[1]),
        pltpu.make_async_copy(x_ref.at[0], xv.at[0], load_sem.at[2]),
        pltpu.make_async_copy(w_ref, wv, load_sem.at[3]),
        pltpu.make_async_copy(cot_ref, cotv, load_sem.at[4]),
    ]

    pl.semaphore_wait(barrier, C - 1 + dp + jnp.where(seg > 0, 1, 0))

    def send_values(h):
        for r in range(1, C):
            pltpu.make_async_remote_copy(
                src_ref=x_ref.at[2, :, cols(h)],
                dst_ref=kv.at[h, 1, pl.ds(r * count, count), :],
                send_sem=kv_send, recv_sem=kv_recv.at[h],
                device_id=ring[r - 1], device_id_type=MESH,
            ).start()

    def send_keys(h):
        for r in range(1, C):
            pltpu.make_async_remote_copy(
                src_ref=kv.at[h, 0, pl.ds(0, count), :],
                dst_ref=kv.at[h, 0, pl.ds(r * count, count), :],
                send_sem=kv_send, recv_sem=kv_recv.at[h],
                device_id=ring[r - 1], device_id_type=MESH,
            ).start()

    lead = min(LEAD, early - 1)

    @pl.loop(0, lead)
    def _(h):
        send_values(h)

    @pl.loop(0, dp)
    def _(d):
        tell(dp_sem, {"dp": d})

    for load in loads[:3]:
        load.start()

    @pl.loop(0, heads)
    def _(h):
        pltpu.make_async_copy(x_ref.at[2, :, cols(h)], kv.at[h, 1, pl.ds(0, count), :], v_sem).start()


    gain_copy = pltpu.make_async_remote_copy(
        src_ref=gain_ref, dst_ref=gains, send_sem=g_send, recv_sem=g_recv,
        device_id=before, device_id_type=MESH,
    )

    @pl.when(seg > 0)
    def _():
        tell(in_sem, before)
        gain_copy.start()

    @pl.when(seg < S - 1)
    def _():
        pl.semaphore_wait(in_sem, 1)

    @pl.when(seg == S - 2)
    def _():
        tell(down_sem, before)

    @pl.when(seg == 1)
    def _():
        tell(up_sem, after)

    @pl.when(seg < S - 2)
    def _():
        pl.semaphore_wait(down_sem, 1)

        @pl.when(seg > 0)
        def _():
            tell(down_sem, before)

    @pl.when(seg == 0)
    def _():
        gain_copy.start()

    @pl.when(seg > 1)
    def _():
        pl.semaphore_wait(up_sem, 1)

        @pl.when(seg < S - 1)
        def _():
            tell(up_sem, after)

    @pl.when(dp < D - 1)
    def _():
        pl.semaphore_wait(dp_sem, D - 1 - dp)

    for who in ring:
        tell(met_sem, who)
    own = kv.at[:, 1, pl.ds(0, count), :]
    pltpu.make_async_copy(own, own, v_sem).wait()

    for load in loads[3:]:
        load.start()

    def hand_over(source, which, h, send=b_send, recv=b_recv):
        pltpu.make_async_remote_copy(
            src_ref=source, dst_ref=direct.at[heads - 1 - h, which, pl.ds(0, count), :],
            send_sem=send, recv_sem=recv, device_id=after, device_id_type=MESH,
        ).start()

    @pl.loop(early, heads)
    def _(h):
        hand_over(kv.at[h, 1, pl.ds(0, count), :], 1, h)

    loads[0].wait()
    pos = jnp.transpose(jnp.broadcast_to(posv[...], (hd, count)))
    s, c = sincos(rope_angles(pos))
    lane = lax.broadcasted_iota(jnp.int32, (count, hd), 1)
    cosv[...] = c
    sinv[...] = jnp.where(lane < hd // 2, -s, s)

    tbuf[0] = jnp.full((8, hd), t_ref[0, 0].astype(jnp.float32), jnp.float32)
    for r in range(1, D):
        pltpu.make_async_remote_copy(
            src_ref=tbuf.at[0], dst_ref=tbuf.at[r], send_sem=t_send, recv_sem=t_recv,
            device_id=clips[r - 1], device_id_type=MESH,
        ).start()

    def inverse_norm(which):
        def add(h, acc):
            x = xv[which, :, cols(h)].astype(jnp.float32)
            return acc + x * x

        acc = lax.fori_loop(0, heads, add, jnp.zeros((count, hd), jnp.float32))
        mean = jnp.sum(acc, axis=1, keepdims=True) / (heads * hd)
        return lax.rsqrt(mean + 1e-06)

    def turned(which, h, inv):
        x = xv[which, :, cols(h)].astype(jnp.float32)
        x = x * inv * gains[which : which + 1, cols(h)]
        return (x * cosv[...] + pltpu.roll(x, hd // 2, 1) * sinv[...]).astype(jnp.bfloat16)

    loads[1].wait()
    inv_k = inverse_norm(1)
    loads[2].wait()
    inv_q = inverse_norm(0)
    gain_copy.wait_recv()

    def forward(slot, sems, send=bx_send):
        for which in range(2):
            for r in range(1, C):
                pltpu.make_async_remote_copy(
                    src_ref=direct.at[slot, which, pl.ds(0, count), :],
                    dst_ref=direct.at[slot, which, pl.ds(r * count, count), :],
                    send_sem=send, recv_sem=sems[which],
                    device_id=ring[r - 1], device_id_type=MESH,
                ).start()

    @pl.loop(0, mine)
    def _(h):
        kv[h, 0, 0:count, :] = turned(1, h, inv_k)
        send_keys(h)

        @pl.when(h + lead < mine)
        def _():
            send_values(h + lead)

    @pl.loop(early, heads)
    def _(h):
        kv[h, 0, 0:count, :] = turned(1, h, inv_k)
        qbuf[h] = turned(0, h, inv_q)
        hand_over(kv.at[h, 0, pl.ds(0, count), :], 0, h)
        hand_over(qbuf.at[h], 2, h)

    spare = early - 1

    @pl.when(give)
    def _():
        kv[spare, 0, 0:count, :] = turned(1, spare, inv_k)
        qbuf[spare] = turned(0, spare, inv_q)
        hand_over(kv.at[spare, 1, pl.ds(0, count), :], 1, spare, e_send, e_recv)
        hand_over(kv.at[spare, 0, pl.ds(0, count), :], 0, spare, e_send, e_recv)
        hand_over(qbuf.at[spare], 2, spare, e_send, e_recv)

    @pl.loop(0, mine)
    def _(h):
        qbuf[h] = turned(0, h, inv_q)

    half = freqs // 2
    decay = -math.log(10000.0) / half
    index = lax.broadcasted_iota(jnp.int32, (half, hd), 0).astype(jnp.float32)
    es, ec = sincos(tbuf[0, 0:1, :] * jnp.exp(index * decay))
    loads[3].wait()

    @pl.loop(0, heads)
    def _(h):
        terms = wv[0:half, cols(h)] * ec + wv[half:freqs, cols(h)] * es
        gate[pl.ds(h, 1), :] = jnp.sum(terms, axis=0, keepdims=True)

    if D > 1:
        others = tbuf.at[pl.ds(1, D - 1)]
        pltpu.make_async_copy(others, others, t_recv).wait()
    at = lax.broadcasted_iota(jnp.int32, (rows, hd), 0) + me * rows
    freq = jnp.exp((at % half).astype(jnp.float32) * decay)
    for j in range(D):
        s, c = sincos(tbuf[j, 0:1, :] * freq)
        emb[j] = jnp.where(at < half, c, s)
    loads[4].wait()

    scale = 1.0 / hd**0.5

    def weigh(queries, keys):
        scores = lax.dot_general(
            queries, keys, (((1,), (1,)), ((), ())), preferred_element_type=jnp.float32
        ) * scale
        expo = jnp.exp(scores - jnp.max(scores, axis=1, keepdims=True))
        return expo.astype(jnp.bfloat16), jnp.sum(expo, axis=1, keepdims=True)

    def attend(h):
        arrived = kv.at[h, :, pl.ds(count, (C - 1) * count), :]
        pltpu.make_async_copy(arrived, arrived, kv_recv.at[h]).wait()
        weights, norm = weigh(qbuf[h], kv[h, 0])
        mixed = jnp.dot(weights, kv[h, 1], preferred_element_type=jnp.float32)
        abuf[h] = (mixed / norm).astype(jnp.bfloat16)
        pltpu.make_async_remote_copy(
            src_ref=abuf.at[h], dst_ref=rbuf.at[h], send_sem=a_send, recv_sem=a_recv.at[h // GROUP],
            device_id=after, device_id_type=MESH,
        ).start()

    def use(h, attn):
        out_ref[:, cols(h)] = (attn * gate[pl.ds(h, 1), :]).astype(jnp.bfloat16)
        cot = cotv[:, cols(h)].astype(jnp.float32)
        return jnp.sum(attn * cot, axis=0, keepdims=True)

    def finish(g):
        some = rbuf.at[pl.ds(g * GROUP, GROUP)]
        pltpu.make_async_copy(some, some, a_recv.at[g]).wait()
        for i in range(GROUP):
            h = g * GROUP + i
            part[0, pl.ds(h, 1), :] = use(h, rbuf[h].astype(jnp.float32))

    @pl.loop(0, mine)
    def _(h):
        attend(h)

        @pl.when(h == FORWARD_AT)
        def _():
            here = direct.at[pl.ds(0, most), :, pl.ds(0, count), :]
            pltpu.make_async_copy(here, here, b_recv).wait()

            @pl.when(take)
            def _():
                more = direct.at[most, :, pl.ds(0, count), :]
                pltpu.make_async_copy(more, more, e_recv).wait()
                forward(most, (ex_recv, ex_recv), ex_send)

            @pl.loop(early, heads - 1)
            def _(g):
                slot = heads - 1 - g
                forward(slot, (bx_recv.at[slot - 1], bx_recv.at[slot - 1]))

        @pl.when(jnp.logical_and(lax.rem(h, GROUP) == GROUP - 1, h >= LAG * GROUP))
        def _():
            finish(h // GROUP - LAG)

    groups = early // GROUP

    @pl.loop(mine // GROUP - LAG, first // GROUP)
    def _(g):
        finish(g)

    for r in range(1, C):
        pltpu.make_async_remote_copy(
            src_ref=part.at[0], dst_ref=part.at[r], send_sem=p_send, recv_sem=p_recv,
            device_id=ring[r - 1], device_id_type=MESH,
        ).start()

    forward(0, (bx_recv.at[most - 1], bx_recv.at[most]))

    def direct_head(h, sem):
        slot = heads - 1 - h
        arrived = direct.at[slot, pl.ds(0, 2), pl.ds(count, (C - 1) * count), :]
        pltpu.make_async_copy(arrived, arrived, sem).wait()
        weights, norm = weigh(direct[slot, 2, 0:count, :], direct[slot, 0])
        mixed = jnp.dot(weights, direct[slot, 1], preferred_element_type=jnp.float32)
        late[0, pl.ds(h - first, 1), :] = use(h, mixed / norm)

    @pl.when(take)
    def _():
        direct_head(spare, ex_recv)

    @pl.loop(early, heads - 1)
    def _(h):
        direct_head(h, bx_recv.at[heads - 2 - h])

    def results(g, size):
        some = rbuf.at[pl.ds(g * GROUP, size)]
        pltpu.make_async_copy(some, some, a_recv.at[g]).wait()
        for i in range(size):
            h = g * GROUP + i
            late[0, pl.ds(h - first, 1), :] = use(h, rbuf[h].astype(jnp.float32))

    @pl.loop(first // GROUP, groups - 1)
    def _(g):
        results(g, GROUP)

    @pl.when(take)
    def _():
        results(groups - 1, GROUP - 1)

    @pl.when(jnp.logical_not(take))
    def _():
        results(groups - 1, GROUP)

    pl.semaphore_wait(met_sem, C - 1)
    order = sorted(range(1, n), key=lambda r: (r % D == 0) + (r < D or r > n - D))

    def share(rows_of, send, recv):
        for r in order:
            pltpu.make_async_remote_copy(
                src_ref=rows_of.at[0], dst_ref=rows_of.at[r], send_sem=send, recv_sem=recv,
                device_id=peers[r - 1], device_id_type=MESH,
            ).start()

    share(late, l_send, l_recv)
    if C > 1:
        others = part.at[pl.ds(1, C - 1)]
        pltpu.make_async_copy(others, others, p_recv).wait()
    acc = part[0]
    for r in range(1, C):
        acc = acc + part[r]
    total[0] = acc
    for r in range(1, D):
        pltpu.make_async_remote_copy(
            src_ref=total.at[0], dst_ref=total.at[r], send_sem=c_send, recv_sem=c_recv,
            device_id=clips[r - 1], device_id_type=MESH,
        ).start()

    final = slice((heads - 1) * hd, heads * hd)
    arrived = direct.at[0, 0, pl.ds(count, (C - 1) * count), :]
    pltpu.make_async_copy(arrived, arrived, bx_recv.at[most - 1]).wait()
    weights, norm = weigh(direct[0, 2, 0:count, :], direct[0, 0])
    inverse = 1.0 / norm
    cot = cotv[:, final].astype(jnp.float32) * inverse
    arrived = direct.at[0, 1, pl.ds(count, (C - 1) * count), :]
    pltpu.make_async_copy(arrived, arrived, bx_recv.at[most]).wait()
    mixed = jnp.dot(weights, direct[0, 1], preferred_element_type=jnp.float32)
    last[0] = jnp.sum(mixed * cot, axis=0, keepdims=True)
    share(last, m_send, m_recv)
    out_ref[:, final] = (mixed * inverse * gate[heads - 1 : heads, :]).astype(jnp.bfloat16)


    gain_copy.wait_send()
    if D > 1:
        others = tbuf.at[pl.ds(1, D - 1)]
        pltpu.make_async_copy(others, others, t_send).wait()
        others = total.at[pl.ds(1, D - 1)]
        pltpu.make_async_copy(others, others, c_recv).wait()
        pltpu.make_async_copy(others, others, c_send).wait()
    if C > 1:
        others = part.at[pl.ds(1, C - 1)]
        pltpu.make_async_copy(others, others, p_send).wait()

    @pl.loop(0, first)
    def _(h):
        acc = emb[0] * total[0, pl.ds(h, 1), :]
        for j in range(1, D):
            acc = acc + emb[j] * total[j, pl.ds(h, 1), :]
        grad_ref[:, cols(h)] = acc

    def drain(number):
        sent = kv.at[pl.ds(0, number), :, pl.ds(count, (C - 1) * count), :]
        pltpu.make_async_copy(sent, sent, kv_send).wait()
        sent = abuf.at[pl.ds(0, number)]
        pltpu.make_async_copy(sent, sent, a_send).wait()

    @pl.when(give)
    def _():
        drain(early - 1)
        sent = direct.at[most, :, pl.ds(0, count), :]
        pltpu.make_async_copy(sent, sent, e_send).wait()

    @pl.when(jnp.logical_not(give))
    def _():
        drain(early)

    @pl.when(take)
    def _():
        sent = direct.at[most, pl.ds(0, 2), pl.ds(count, (C - 1) * count), :]
        pltpu.make_async_copy(sent, sent, ex_send).wait()

    sent = direct.at[pl.ds(0, most), :, pl.ds(0, count), :]
    pltpu.make_async_copy(sent, sent, b_send).wait()
    sent = direct.at[pl.ds(0, most), pl.ds(0, 2), pl.ds(count, (C - 1) * count), :]
    pltpu.make_async_copy(sent, sent, bx_send).wait()

    def grads(rows_of, recv, send, start):
        others = rows_of.at[pl.ds(1, n - 1)]
        pltpu.make_async_copy(others, others, recv).wait()
        sums = []
        for j in range(D):
            acc = rows_of[j]
            for c in range(1, C):
                acc = acc + rows_of[j + c * D]
            sums.append(acc)
        for i in range(rows_of.shape[1]):
            acc = emb[0] * sums[0][i : i + 1, :]
            for j in range(1, D):
                acc = acc + emb[j] * sums[j][i : i + 1, :]
            grad_ref[:, (start + i) * hd : (start + i + 1) * hd] = acc
        pltpu.make_async_copy(others, others, send).wait()

    grads(late, l_recv, l_send, first)
    grads(last, m_recv, m_send, heads - 1)


def store(attn_ref, grad_ref, out_ref, grads_ref, out_sem, grad_sem):
    copies = [
        pltpu.make_async_copy(attn_ref, out_ref, out_sem),
        pltpu.make_async_copy(grad_ref, grads_ref, grad_sem),
    ]
    for copy in copies:
        copy.start()
    for copy in copies:
        copy.wait()


def local(S, C, D, qkv, qk_gain, mod_weight, positions, timesteps, cotangent):
    count, _, width = qkv.shape[2:]
    freqs = mod_weight.shape[1]
    heads = width // HEAD_DIM
    n = C * D
    rows = freqs // n
    hd = HEAD_DIM
    most = DIRECT
    early = heads - most
    first = FIRST
    if S < 3 or n < 2 or early % GROUP or first % GROUP or first + GROUP > early or FORWARD_AT >= early:
        raise ValueError("unsupported mesh")
    bf, f32 = jnp.bfloat16, jnp.float32
    vmem = pl.BlockSpec(memory_space=pltpu.VMEM)
    hbm = pl.BlockSpec(memory_space=pltpu.HBM)
    dma = pltpu.SemaphoreType.DMA
    regular = pltpu.SemaphoreType.REGULAR
    pin = functools.partial(pltpu.with_memory_space_constraint, memory_space=pltpu.HBM)
    attn, grad = pl.pallas_call(
        functools.partial(body, S, C, D, heads, freqs),
        out_shape=(
            jax.ShapeDtypeStruct((count, width), bf),
            jax.ShapeDtypeStruct((rows, width), f32),
        ),
        in_specs=[hbm] * 4 + [pl.BlockSpec(memory_space=pltpu.SMEM), hbm],
        out_specs=(vmem, vmem),
        scratch_shapes=[
            pltpu.VMEM((2, count, width), bf),
            pltpu.VMEM((freqs, width), f32),
            pltpu.VMEM((count, width), bf),
            pltpu.VMEM((heads, 2, C * count, hd), bf),
            pltpu.VMEM((heads, count, hd), bf),
            pltpu.VMEM((heads, count, hd), bf),
            pltpu.VMEM((heads, count, hd), bf),
            pltpu.VMEM((most + 1, 3, C * count, hd), bf),
            pltpu.VMEM((2, width), f32),
            pltpu.VMEM((1, count), jnp.int32),
            pltpu.VMEM((D, 8, hd), f32),
            pltpu.VMEM((-(-heads // 8) * 8, hd), f32),
            pltpu.VMEM((D, rows, hd), f32),
            pltpu.VMEM((count, hd), f32),
            pltpu.VMEM((count, hd), f32),
            pltpu.VMEM((C, first, hd), f32),
            pltpu.VMEM((D, first, hd), f32),
            pltpu.VMEM((n, heads - 1 - first, hd), f32),
            pltpu.VMEM((n, 1, hd), f32),
            dma((5,)), dma,
            dma, dma((early,)), dma, dma((early // GROUP,)),
            dma, dma, dma, dma, dma, dma, dma, dma, dma, dma, dma, dma,
            dma, dma, dma, dma((most + 1,)), dma, dma, dma, dma,
            regular, regular, regular, regular, regular,
        ],
        compiler_params=pltpu.CompilerParams(
            collective_id=0, has_side_effects=True, vmem_limit_bytes=VMEM_LIMIT if C <= 2 else 60 << 20
        ),
    )(
        pin(jnp.moveaxis(qkv[0, 0], 1, 0)),
        pin(qk_gain[0]),
        pin(mod_weight[0]),
        pin(positions),
        timesteps,
        pin(cotangent[0, 0]),
    )
    anywhere = pl.BlockSpec(memory_space=pl.ANY)
    attn_out, gate_grad = pl.pallas_call(
        store,
        out_shape=(
            jax.ShapeDtypeStruct((count, width), bf),
            jax.ShapeDtypeStruct((rows, width), f32),
        ),
        in_specs=[anywhere, anywhere],
        out_specs=(anywhere, anywhere),
        scratch_shapes=[dma, dma],
        compiler_params=pltpu.CompilerParams(vmem_limit_bytes=4 << 20),
    )(attn, grad)
    return attn_out[None, None], gate_grad[None]


def solution(mesh):
    sizes = mesh.shape
    return jax.shard_map(
        functools.partial(local, sizes["segment"], sizes["ctx"], sizes["dp"]),
        mesh=mesh,
        in_specs=(
            P("segment", "dp", "ctx", None, None),
            P("segment", None, None),
            P("segment", None, None),
            P("dp", "ctx"),
            P("segment", "dp"),
            P("segment", "dp", "ctx", None),
        ),
        out_specs=(P("segment", "dp", "ctx", None), P("segment", ("ctx", "dp"), None)),
        check_vma=False,
    )
```

```python
import functools
import math

import jax
import jax.numpy as jnp
from jax import lax
from jax.experimental import pallas as pl
from jax.experimental.pallas import tpu as pltpu
from jax.sharding import PartitionSpec as P

HEAD_DIM = 128
GRID_ROWS = 45
GRID_COLS = 80
MESH = pl.DeviceIdType.MESH
LEAD = 12
GROUP = 3
LAG = 3
DIRECT = 5
FIRST = 9
GIVER = 0
FORWARD_AT = 8
VMEM_LIMIT = 24 << 20


def sincos(angle):
    turns = jnp.floor(angle * (2.0 / math.pi) + 0.5)
    quad = turns.astype(jnp.int32)
    r = angle - turns * 1.5703125
    r = r - turns * 4.837512969970703125e-4
    r = r - turns * 7.549789948768648e-8
    z = r * r
    sine = r + r * z * (-1.6666654611e-1 + z * (8.3321608736e-3 - z * 1.9515295891e-4))
    cosine = 1.0 - 0.5 * z + z * z * (
        4.166664568298827e-2 + z * (-1.388731625493765e-3 + z * 2.443315711809948e-5)
    )
    swap = (quad & 1) == 1
    s = jnp.where(swap, cosine, sine)
    c = jnp.where(swap, sine, cosine)
    s = jnp.where((quad & 2) == 2, -s, s)
    c = jnp.where(((quad + 1) & 2) == 2, -c, c)
    return s, c


def rope_angles(pos):
    count, hd = pos.shape
    half = hd // 2
    side = hd // 6
    first = half - 2 * side
    pair = lax.broadcasted_iota(jnp.int32, (8, hd), 1) % half
    group = jnp.where(pair < first, 0, jnp.where(pair < first + side, 1, 2))
    offset = jnp.where(group == 0, 0, jnp.where(group == 1, first, first + side))
    pairs_in = jnp.where(group == 0, first, side).astype(jnp.float32)
    freq = jnp.exp((pair - offset).astype(jnp.float32) / pairs_in * -math.log(10000.0))[0:1]
    group = group[0:1]
    frame = (pos // (GRID_ROWS * GRID_COLS)).astype(jnp.float32)
    row = (pos // GRID_COLS % GRID_ROWS).astype(jnp.float32)
    col = (pos % GRID_COLS).astype(jnp.float32)
    return jnp.where(group == 0, frame, jnp.where(group == 1, row, col)) * freq


def body(
    S, C, D, heads, freqs,
    x_ref, gain_ref, w_ref, pos_ref, t_ref, cot_ref,
    out_ref, grad_ref,
    xv, wv, cotv, kv, qbuf, abuf, rbuf, direct, gains, posv, tbuf, gate, emb, cosv, sinv,
    part, total, late, last, ubuf, ures,
    load_sem, v_sem, kv_send, kv_recv, a_send, a_recv, g_send, g_recv, t_send, t_recv,
    p_send, p_recv, c_send, c_recv, l_send, l_recv, m_send, m_recv,
    b_send, b_recv, bx_send, bx_recv, e_send, e_recv, ex_send, ex_recv, u_send, u_recv, ur_send, in_sem, down_sem, up_sem, met_sem, dp_sem,
):
    n = C * D
    count = x_ref.shape[1]
    rows = freqs // n
    hd = HEAD_DIM
    first = part.shape[1]
    seg = lax.axis_index("segment")
    ctx = lax.axis_index("ctx")
    dp = lax.axis_index("dp")
    me = ctx * D + dp
    after = {"segment": lax.rem(seg + 1, S)}
    before = {"segment": lax.rem(seg + S - 1, S)}
    most = direct.shape[0] - 1
    early = heads - most
    edge = dp == D - 1
    give = jnp.logical_and(seg == GIVER, edge)
    take = jnp.logical_and(seg == GIVER + 1, edge)
    mine = early - jnp.where(give, 1, 0)
    swap = jnp.logical_and(dp == D - 2, C == 2)
    host = jnp.logical_and(swap, ctx == 0)
    guest = jnp.logical_and(swap, ctx == 1)
    low = jnp.where(swap, 1, 0)
    peers = []
    for r in range(1, n):
        p = lax.rem(me + r, n)
        peers.append({"ctx": p // D, "dp": lax.rem(p, D)})
    ring = [{"ctx": lax.rem(ctx + r, C)} for r in range(1, C)]
    clips = [{"dp": lax.rem(dp + r, D)} for r in range(1, D)]

    def cols(h):
        return pl.ds(pl.multiple_of(h * hd, hd), hd)

    def tell(sem, who):
        pl.semaphore_signal(sem, inc=1, device_id=who, device_id_type=MESH)

    barrier = pltpu.get_barrier_semaphore()
    for who in ring:
        tell(barrier, who)

    pairs = D == 4
    if pairs:
        @pl.when(dp < 2)
        def _():
            tell(barrier, {"dp": dp + 2})

        @pl.when(lax.rem(dp, 2) == 1)
        def _():
            tell(barrier, {"dp": dp - 1})

        met = jnp.where(dp >= 2, 1, 0) + jnp.where(lax.rem(dp, 2) == 0, 1, 0)
    else:
        @pl.loop(dp + 1, D)
        def _(d):
            tell(barrier, {"dp": d})

        met = dp

    @pl.when(seg < S - 1)
    def _():
        tell(barrier, after)

    loads = [
        pltpu.make_async_copy(pos_ref, posv, load_sem.at[0]),
        pltpu.make_async_copy(x_ref.at[1], xv.at[1], load_sem.at[1]),
        pltpu.make_async_copy(x_ref.at[0], xv.at[0], load_sem.at[2]),
        pltpu.make_async_copy(w_ref, wv, load_sem.at[3]),
        pltpu.make_async_copy(cot_ref, cotv, load_sem.at[4]),
    ]

    pl.semaphore_wait(barrier, C - 1 + met + jnp.where(seg > 0, 1, 0))

    def send_values(h):
        for r in range(1, C):
            pltpu.make_async_remote_copy(
                src_ref=x_ref.at[2, :, cols(h)],
                dst_ref=kv.at[h, 1, pl.ds(r * count, count), :],
                send_sem=kv_send, recv_sem=kv_recv.at[h],
                device_id=ring[r - 1], device_id_type=MESH,
            ).start()

    def send_keys(h):
        for r in range(1, C):
            pltpu.make_async_remote_copy(
                src_ref=kv.at[h, 0, pl.ds(0, count), :],
                dst_ref=kv.at[h, 0, pl.ds(r * count, count), :],
                send_sem=kv_send, recv_sem=kv_recv.at[h],
                device_id=ring[r - 1], device_id_type=MESH,
            ).start()

    lead = min(LEAD, early - 2)

    @pl.loop(low, low + lead)
    def _(h):
        send_values(h)

    if pairs:
        @pl.when(dp == 2)
        def _():
            tell(dp_sem, {"dp": dp - 2})
            tell(dp_sem, {"dp": dp + 1})
    else:
        @pl.loop(0, dp)
        def _(d):
            tell(dp_sem, {"dp": d})

    for load in loads[:3]:
        load.start()

    @pl.loop(0, heads)
    def _(h):
        pltpu.make_async_copy(x_ref.at[2, :, cols(h)], kv.at[h, 1, pl.ds(0, count), :], v_sem).start()


    gain_copy = pltpu.make_async_remote_copy(
        src_ref=gain_ref, dst_ref=gains, send_sem=g_send, recv_sem=g_recv,
        device_id=before, device_id_type=MESH,
    )

    @pl.when(seg > 0)
    def _():
        tell(in_sem, before)
        gain_copy.start()

    @pl.when(seg < S - 1)
    def _():
        pl.semaphore_wait(in_sem, 1)

    @pl.when(seg == S - 2)
    def _():
        tell(down_sem, before)

    @pl.when(seg == 1)
    def _():
        tell(up_sem, after)

    @pl.when(seg < S - 2)
    def _():
        pl.semaphore_wait(down_sem, 1)

        @pl.when(seg > 0)
        def _():
            tell(down_sem, before)

    @pl.when(seg == 0)
    def _():
        gain_copy.start()

    @pl.when(seg > 1)
    def _():
        pl.semaphore_wait(up_sem, 1)

        @pl.when(seg < S - 1)
        def _():
            tell(up_sem, after)

    if pairs:
        pl.semaphore_wait(dp_sem, 1)

        @pl.when(dp == 0)
        def _():
            tell(dp_sem, {"dp": dp + 1})
            tell(dp_sem, {"dp": dp + 2})
    else:
        @pl.when(dp < D - 1)
        def _():
            pl.semaphore_wait(dp_sem, D - 1 - dp)

    for who in ring:
        tell(met_sem, who)
    own = kv.at[:, 1, pl.ds(0, count), :]
    pltpu.make_async_copy(own, own, v_sem).wait()

    for load in loads[3:]:
        load.start()

    def hand_over(source, which, h, send=b_send, recv=b_recv):
        pltpu.make_async_remote_copy(
            src_ref=source, dst_ref=direct.at[heads - 1 - h, which, pl.ds(0, count), :],
            send_sem=send, recv_sem=recv, device_id=after, device_id_type=MESH,
        ).start()

    @pl.loop(early, heads)
    def _(h):
        hand_over(kv.at[h, 1, pl.ds(0, count), :], 1, h)

    loads[0].wait()
    pos = jnp.transpose(jnp.broadcast_to(posv[...], (hd, count)))
    s, c = sincos(rope_angles(pos))
    lane = lax.broadcasted_iota(jnp.int32, (count, hd), 1)
    cosv[...] = c
    sinv[...] = jnp.where(lane < hd // 2, -s, s)

    tbuf[0] = jnp.full((8, hd), t_ref[0, 0].astype(jnp.float32), jnp.float32)
    for r in range(1, D):
        pltpu.make_async_remote_copy(
            src_ref=tbuf.at[0], dst_ref=tbuf.at[r], send_sem=t_send, recv_sem=t_recv,
            device_id=clips[r - 1], device_id_type=MESH,
        ).start()

    def inverse_norm(which):
        def add(h, acc):
            x = xv[which, :, cols(h)].astype(jnp.float32)
            return acc + x * x

        acc = lax.fori_loop(0, heads, add, jnp.zeros((count, hd), jnp.float32))
        mean = jnp.sum(acc, axis=1, keepdims=True) / (heads * hd)
        return lax.rsqrt(mean + 1e-06)

    def turned(which, h, inv):
        x = xv[which, :, cols(h)].astype(jnp.float32)
        x = x * inv * gains[which : which + 1, cols(h)]
        return (x * cosv[...] + pltpu.roll(x, hd // 2, 1) * sinv[...]).astype(jnp.bfloat16)

    loads[1].wait()
    inv_k = inverse_norm(1)
    loads[2].wait()
    inv_q = inverse_norm(0)
    gain_copy.wait_recv()

    def forward(slot, sems, send=bx_send):
        for which in range(2):
            for r in range(1, C):
                pltpu.make_async_remote_copy(
                    src_ref=direct.at[slot, which, pl.ds(0, count), :],
                    dst_ref=direct.at[slot, which, pl.ds(r * count, count), :],
                    send_sem=send, recv_sem=sems[which],
                    device_id=ring[r - 1], device_id_type=MESH,
                ).start()

    @pl.when(swap)
    def _():
        kv[0, 0, 0:count, :] = turned(1, 0, inv_k)
        qbuf[0] = turned(0, 0, inv_q)

    @pl.when(guest)
    def _():
        for i, source in enumerate((kv.at[0, 0, pl.ds(0, count), :], kv.at[0, 1, pl.ds(0, count), :], qbuf.at[0])):
            pltpu.make_async_remote_copy(
                src_ref=source, dst_ref=ubuf.at[i], send_sem=u_send, recv_sem=u_recv,
                device_id=ring[0], device_id_type=MESH,
            ).start()

    @pl.loop(low, mine)
    def _(h):
        kv[h, 0, 0:count, :] = turned(1, h, inv_k)
        send_keys(h)

        @pl.when(h + lead < mine)
        def _():
            send_values(h + lead)

    @pl.loop(early, heads)
    def _(h):
        kv[h, 0, 0:count, :] = turned(1, h, inv_k)
        qbuf[h] = turned(0, h, inv_q)
        hand_over(kv.at[h, 0, pl.ds(0, count), :], 0, h)
        hand_over(qbuf.at[h], 2, h)

    spare = early - 1

    @pl.when(give)
    def _():
        kv[spare, 0, 0:count, :] = turned(1, spare, inv_k)
        qbuf[spare] = turned(0, spare, inv_q)
        hand_over(kv.at[spare, 1, pl.ds(0, count), :], 1, spare, e_send, e_recv)
        hand_over(kv.at[spare, 0, pl.ds(0, count), :], 0, spare, e_send, e_recv)
        hand_over(qbuf.at[spare], 2, spare, e_send, e_recv)

    @pl.loop(low, mine)
    def _(h):
        qbuf[h] = turned(0, h, inv_q)

    half = freqs // 2
    decay = -math.log(10000.0) / half
    index = lax.broadcasted_iota(jnp.int32, (half, hd), 0).astype(jnp.float32)
    es, ec = sincos(tbuf[0, 0:1, :] * jnp.exp(index * decay))
    loads[3].wait()

    @pl.loop(0, heads)
    def _(h):
        terms = wv[0:half, cols(h)] * ec + wv[half:freqs, cols(h)] * es
        gate[pl.ds(h, 1), :] = jnp.sum(terms, axis=0, keepdims=True)

    if D > 1:
        others = tbuf.at[pl.ds(1, D - 1)]
        pltpu.make_async_copy(others, others, t_recv).wait()
    at = lax.broadcasted_iota(jnp.int32, (rows, hd), 0) + me * rows
    freq = jnp.exp((at % half).astype(jnp.float32) * decay)
    for j in range(D):
        s, c = sincos(tbuf[j, 0:1, :] * freq)
        emb[j] = jnp.where(at < half, c, s)
    loads[4].wait()

    scale = 1.0 / hd**0.5

    def weigh(queries, keys):
        scores = lax.dot_general(
            queries, keys, (((1,), (1,)), ((), ())), preferred_element_type=jnp.float32
        ) * scale
        expo = jnp.exp(scores - jnp.max(scores, axis=1, keepdims=True))
        return expo.astype(jnp.bfloat16), jnp.sum(expo, axis=1, keepdims=True)

    def attend(h):
        arrived = kv.at[h, :, pl.ds(count, (C - 1) * count), :]
        pltpu.make_async_copy(arrived, arrived, kv_recv.at[h]).wait()
        weights, norm = weigh(qbuf[h], kv[h, 0])
        mixed = jnp.dot(weights, kv[h, 1], preferred_element_type=jnp.float32)
        abuf[h] = (mixed / norm).astype(jnp.bfloat16)
        pltpu.make_async_remote_copy(
            src_ref=abuf.at[h], dst_ref=rbuf.at[h], send_sem=a_send, recv_sem=a_recv.at[h // GROUP],
            device_id=after, device_id_type=MESH,
        ).start()

    def use(h, attn):
        out_ref[:, cols(h)] = (attn * gate[pl.ds(h, 1), :]).astype(jnp.bfloat16)
        cot = cotv[:, cols(h)].astype(jnp.float32)
        return jnp.sum(attn * cot, axis=0, keepdims=True)

    def finish(g):
        some = rbuf.at[pl.ds(g * GROUP, GROUP)]
        pltpu.make_async_copy(some, some, a_recv.at[g]).wait()
        for i in range(GROUP):
            h = g * GROUP + i
            part[0, pl.ds(h, 1), :] = use(h, rbuf[h].astype(jnp.float32))

    @pl.when(host)
    def _():
        some = ubuf.at[pl.ds(0, 3)]
        pltpu.make_async_copy(some, some, u_recv).wait()
        kv[0, 0, count : 2 * count, :] = ubuf[0]
        kv[0, 1, count : 2 * count, :] = ubuf[1]
        ubuf[3] = qbuf[0]

        @pl.loop(0, 2)
        def _(i):
            weights, norm = weigh(ubuf[2 + i], kv[0, 0])
            mixed = jnp.dot(weights, kv[0, 1], preferred_element_type=jnp.float32)
            ures[i] = (mixed / norm).astype(jnp.bfloat16)
            pltpu.make_async_remote_copy(
                src_ref=ures.at[i], dst_ref=rbuf.at[0], send_sem=ur_send, recv_sem=a_recv.at[0],
                device_id={"segment": after["segment"], "ctx": 1 - i}, device_id_type=MESH,
            ).start()

    @pl.loop(low, mine)
    def _(h):
        attend(h)

        @pl.when(h == FORWARD_AT)
        def _():
            here = direct.at[pl.ds(0, most), :, pl.ds(0, count), :]
            pltpu.make_async_copy(here, here, b_recv).wait()

            @pl.when(take)
            def _():
                more = direct.at[most, :, pl.ds(0, count), :]
                pltpu.make_async_copy(more, more, e_recv).wait()
                forward(most, (ex_recv, ex_recv), ex_send)

            @pl.loop(early, heads - 1)
            def _(g):
                slot = heads - 1 - g
                forward(slot, (bx_recv.at[slot - 1], bx_recv.at[slot - 1]))

        @pl.when(jnp.logical_and(lax.rem(h, GROUP) == GROUP - 1, h >= LAG * GROUP))
        def _():
            finish(h // GROUP - LAG)

    groups = early // GROUP

    @pl.loop(mine // GROUP - LAG, first // GROUP)
    def _(g):
        finish(g)

    for r in range(1, C):
        pltpu.make_async_remote_copy(
            src_ref=part.at[0], dst_ref=part.at[r], send_sem=p_send, recv_sem=p_recv,
            device_id=ring[r - 1], device_id_type=MESH,
        ).start()

    forward(0, (bx_recv.at[most - 1], bx_recv.at[most]))

    def direct_head(h, sem):
        slot = heads - 1 - h
        arrived = direct.at[slot, pl.ds(0, 2), pl.ds(count, (C - 1) * count), :]
        pltpu.make_async_copy(arrived, arrived, sem).wait()
        weights, norm = weigh(direct[slot, 2, 0:count, :], direct[slot, 0])
        mixed = jnp.dot(weights, direct[slot, 1], preferred_element_type=jnp.float32)
        late[0, pl.ds(h - first, 1), :] = use(h, mixed / norm)

    @pl.when(take)
    def _():
        direct_head(spare, ex_recv)

    @pl.loop(early, heads - 1)
    def _(h):
        direct_head(h, bx_recv.at[heads - 2 - h])

    def results(g, size):
        some = rbuf.at[pl.ds(g * GROUP, size)]
        pltpu.make_async_copy(some, some, a_recv.at[g]).wait()
        for i in range(size):
            h = g * GROUP + i
            late[0, pl.ds(h - first, 1), :] = use(h, rbuf[h].astype(jnp.float32))

    @pl.loop(first // GROUP, groups - 1)
    def _(g):
        results(g, GROUP)

    @pl.when(take)
    def _():
        results(groups - 1, GROUP - 1)

    @pl.when(jnp.logical_not(take))
    def _():
        results(groups - 1, GROUP)

    pl.semaphore_wait(met_sem, C - 1)
    order = sorted(range(1, n), key=lambda r: (r % D == 0) + (r < D or r > n - D))

    def share(rows_of, send, recv):
        for r in order:
            pltpu.make_async_remote_copy(
                src_ref=rows_of.at[0], dst_ref=rows_of.at[r], send_sem=send, recv_sem=recv,
                device_id=peers[r - 1], device_id_type=MESH,
            ).start()

    share(late, l_send, l_recv)
    if C > 1:
        others = part.at[pl.ds(1, C - 1)]
        pltpu.make_async_copy(others, others, p_recv).wait()
    acc = part[0]
    for r in range(1, C):
        acc = acc + part[r]
    total[0] = acc
    for r in range(1, D):
        pltpu.make_async_remote_copy(
            src_ref=total.at[0], dst_ref=total.at[r], send_sem=c_send, recv_sem=c_recv,
            device_id=clips[r - 1], device_id_type=MESH,
        ).start()

    final = slice((heads - 1) * hd, heads * hd)
    arrived = direct.at[0, 0, pl.ds(count, (C - 1) * count), :]
    pltpu.make_async_copy(arrived, arrived, bx_recv.at[most - 1]).wait()
    weights, norm = weigh(direct[0, 2, 0:count, :], direct[0, 0])
    inverse = 1.0 / norm
    cot = cotv[:, final].astype(jnp.float32) * inverse
    arrived = direct.at[0, 1, pl.ds(count, (C - 1) * count), :]
    pltpu.make_async_copy(arrived, arrived, bx_recv.at[most]).wait()
    mixed = jnp.dot(weights, direct[0, 1], preferred_element_type=jnp.float32)
    last[0] = jnp.sum(mixed * cot, axis=0, keepdims=True)
    share(last, m_send, m_recv)
    out_ref[:, final] = (mixed * inverse * gate[heads - 1 : heads, :]).astype(jnp.bfloat16)


    gain_copy.wait_send()
    if D > 1:
        others = tbuf.at[pl.ds(1, D - 1)]
        pltpu.make_async_copy(others, others, t_send).wait()
        others = total.at[pl.ds(1, D - 1)]
        pltpu.make_async_copy(others, others, c_recv).wait()
        pltpu.make_async_copy(others, others, c_send).wait()
    if C > 1:
        others = part.at[pl.ds(1, C - 1)]
        pltpu.make_async_copy(others, others, p_send).wait()

    @pl.loop(0, first)
    def _(h):
        acc = emb[0] * total[0, pl.ds(h, 1), :]
        for j in range(1, D):
            acc = acc + emb[j] * total[j, pl.ds(h, 1), :]
        grad_ref[:, cols(h)] = acc

    def drain(number):
        sent = kv.at[pl.ds(0, number), :, pl.ds(count, (C - 1) * count), :]
        pltpu.make_async_copy(sent, sent, kv_send).wait()
        sent = abuf.at[pl.ds(0, number)]
        pltpu.make_async_copy(sent, sent, a_send).wait()

    fewer = jnp.logical_or(give, swap)

    @pl.when(fewer)
    def _():
        drain(early - 1)

    @pl.when(jnp.logical_not(fewer))
    def _():
        drain(early)

    @pl.when(give)
    def _():
        sent = direct.at[most, :, pl.ds(0, count), :]
        pltpu.make_async_copy(sent, sent, e_send).wait()

    @pl.when(guest)
    def _():
        sent = ubuf.at[pl.ds(0, 3)]
        pltpu.make_async_copy(sent, sent, u_send).wait()

    @pl.when(host)
    def _():
        pltpu.make_async_copy(ures, ures, ur_send).wait()

    @pl.when(take)
    def _():
        sent = direct.at[most, pl.ds(0, 2), pl.ds(count, (C - 1) * count), :]
        pltpu.make_async_copy(sent, sent, ex_send).wait()

    sent = direct.at[pl.ds(0, most), :, pl.ds(0, count), :]
    pltpu.make_async_copy(sent, sent, b_send).wait()
    sent = direct.at[pl.ds(0, most), pl.ds(0, 2), pl.ds(count, (C - 1) * count), :]
    pltpu.make_async_copy(sent, sent, bx_send).wait()

    def grads(rows_of, recv, send, start):
        others = rows_of.at[pl.ds(1, n - 1)]
        pltpu.make_async_copy(others, others, recv).wait()
        sums = []
        for j in range(D):
            acc = rows_of[j]
            for c in range(1, C):
                acc = acc + rows_of[j + c * D]
            sums.append(acc)
        for i in range(rows_of.shape[1]):
            acc = emb[0] * sums[0][i : i + 1, :]
            for j in range(1, D):
                acc = acc + emb[j] * sums[j][i : i + 1, :]
            grad_ref[:, (start + i) * hd : (start + i + 1) * hd] = acc
        pltpu.make_async_copy(others, others, send).wait()

    grads(late, l_recv, l_send, first)
    grads(last, m_recv, m_send, heads - 1)


def store(attn_ref, grad_ref, out_ref, grads_ref, out_sem, grad_sem):
    copies = [
        pltpu.make_async_copy(attn_ref, out_ref, out_sem),
        pltpu.make_async_copy(grad_ref, grads_ref, grad_sem),
    ]
    for copy in copies:
        copy.start()
    for copy in copies:
        copy.wait()


def local(S, C, D, qkv, qk_gain, mod_weight, positions, timesteps, cotangent):
    count, _, width = qkv.shape[2:]
    freqs = mod_weight.shape[1]
    heads = width // HEAD_DIM
    n = C * D
    rows = freqs // n
    hd = HEAD_DIM
    most = DIRECT
    early = heads - most
    first = FIRST
    if S < 3 or C < 2 or D < 2 or early % GROUP or first % GROUP or first + GROUP > early or FORWARD_AT >= early:
        raise ValueError("unsupported mesh")
    bf, f32 = jnp.bfloat16, jnp.float32
    vmem = pl.BlockSpec(memory_space=pltpu.VMEM)
    hbm = pl.BlockSpec(memory_space=pltpu.HBM)
    dma = pltpu.SemaphoreType.DMA
    regular = pltpu.SemaphoreType.REGULAR
    pin = functools.partial(pltpu.with_memory_space_constraint, memory_space=pltpu.HBM)
    attn, grad = pl.pallas_call(
        functools.partial(body, S, C, D, heads, freqs),
        out_shape=(
            jax.ShapeDtypeStruct((count, width), bf),
            jax.ShapeDtypeStruct((rows, width), f32),
        ),
        in_specs=[hbm] * 4 + [pl.BlockSpec(memory_space=pltpu.SMEM), hbm],
        out_specs=(vmem, vmem),
        scratch_shapes=[
            pltpu.VMEM((2, count, width), bf),
            pltpu.VMEM((freqs, width), f32),
            pltpu.VMEM((count, width), bf),
            pltpu.VMEM((heads, 2, C * count, hd), bf),
            pltpu.VMEM((heads, count, hd), bf),
            pltpu.VMEM((heads, count, hd), bf),
            pltpu.VMEM((heads, count, hd), bf),
            pltpu.VMEM((most + 1, 3, C * count, hd), bf),
            pltpu.VMEM((2, width), f32),
            pltpu.VMEM((1, count), jnp.int32),
            pltpu.VMEM((D, 8, hd), f32),
            pltpu.VMEM((-(-heads // 8) * 8, hd), f32),
            pltpu.VMEM((D, rows, hd), f32),
            pltpu.VMEM((count, hd), f32),
            pltpu.VMEM((count, hd), f32),
            pltpu.VMEM((C, first, hd), f32),
            pltpu.VMEM((D, first, hd), f32),
            pltpu.VMEM((n, heads - 1 - first, hd), f32),
            pltpu.VMEM((n, 1, hd), f32),
            pltpu.VMEM((4, count, hd), bf),
            pltpu.VMEM((2, count, hd), bf),
            dma((5,)), dma,
            dma, dma((early,)), dma, dma((early // GROUP,)),
            dma, dma, dma, dma, dma, dma, dma, dma, dma, dma, dma, dma,
            dma, dma, dma, dma((most + 1,)), dma, dma, dma, dma, dma, dma, dma,
            regular, regular, regular, regular, regular,
        ],
        compiler_params=pltpu.CompilerParams(
            collective_id=0, has_side_effects=True, vmem_limit_bytes=VMEM_LIMIT if C <= 2 else 60 << 20
        ),
    )(
        pin(jnp.moveaxis(qkv[0, 0], 1, 0)),
        pin(qk_gain[0]),
        pin(mod_weight[0]),
        pin(positions),
        timesteps,
        pin(cotangent[0, 0]),
    )
    anywhere = pl.BlockSpec(memory_space=pl.ANY)
    attn_out, gate_grad = pl.pallas_call(
        store,
        out_shape=(
            jax.ShapeDtypeStruct((count, width), bf),
            jax.ShapeDtypeStruct((rows, width), f32),
        ),
        in_specs=[anywhere, anywhere],
        out_specs=(anywhere, anywhere),
        scratch_shapes=[dma, dma],
        compiler_params=pltpu.CompilerParams(vmem_limit_bytes=4 << 20),
    )(attn, grad)
    return attn_out[None, None], gate_grad[None]


def solution(mesh):
    sizes = mesh.shape
    return jax.shard_map(
        functools.partial(local, sizes["segment"], sizes["ctx"], sizes["dp"]),
        mesh=mesh,
        in_specs=(
            P("segment", "dp", "ctx", None, None),
            P("segment", None, None),
            P("segment", None, None),
            P("dp", "ctx"),
            P("segment", "dp"),
            P("segment", "dp", "ctx", None),
        ),
        out_specs=(P("segment", "dp", "ctx", None), P("segment", ("ctx", "dp"), None)),
        check_vma=False,
    )
```

```python
import functools
import math

import jax
import jax.numpy as jnp
from jax import lax
from jax.experimental import pallas as pl
from jax.experimental.pallas import tpu as pltpu
from jax.sharding import PartitionSpec as P

HEAD_DIM = 128
GRID_ROWS = 45
GRID_COLS = 80
MESH = pl.DeviceIdType.MESH
LEAD = 12
GROUP = 3
LAG = 3
DIRECT = 5
FIRST = 6
FAR = 2
FORWARD_AT = 8
VMEM_LIMIT = 24 << 20


def sincos(angle):
    turns = jnp.floor(angle * (2.0 / math.pi) + 0.5)
    quad = turns.astype(jnp.int32)
    r = angle - turns * 1.5703125
    r = r - turns * 4.837512969970703125e-4
    r = r - turns * 7.549789948768648e-8
    z = r * r
    sine = r + r * z * (-1.6666654611e-1 + z * (8.3321608736e-3 - z * 1.9515295891e-4))
    cosine = 1.0 - 0.5 * z + z * z * (
        4.166664568298827e-2 + z * (-1.388731625493765e-3 + z * 2.443315711809948e-5)
    )
    swap = (quad & 1) == 1
    s = jnp.where(swap, cosine, sine)
    c = jnp.where(swap, sine, cosine)
    s = jnp.where((quad & 2) == 2, -s, s)
    c = jnp.where(((quad + 1) & 2) == 2, -c, c)
    return s, c


def rope_angles(pos):
    count, hd = pos.shape
    half = hd // 2
    side = hd // 6
    first = half - 2 * side
    pair = lax.broadcasted_iota(jnp.int32, (8, hd), 1) % half
    group = jnp.where(pair < first, 0, jnp.where(pair < first + side, 1, 2))
    offset = jnp.where(group == 0, 0, jnp.where(group == 1, first, first + side))
    pairs_in = jnp.where(group == 0, first, side).astype(jnp.float32)
    freq = jnp.exp((pair - offset).astype(jnp.float32) / pairs_in * -math.log(10000.0))[0:1]
    group = group[0:1]
    frame = (pos // (GRID_ROWS * GRID_COLS)).astype(jnp.float32)
    row = (pos // GRID_COLS % GRID_ROWS).astype(jnp.float32)
    col = (pos % GRID_COLS).astype(jnp.float32)
    return jnp.where(group == 0, frame, jnp.where(group == 1, row, col)) * freq


def body(
    S, C, D, heads, freqs,
    x_ref, gain_ref, w_ref, pos_ref, t_ref, cot_ref,
    out_ref, grad_ref,
    xv, wv, cotv, kv, qbuf, abuf, rbuf, direct, gains, posv, tbuf, gate, emb, cosv, sinv,
    part, total, late, last, ubuf, ures,
    load_sem, v_sem, kv_send, kv_recv, a_send, a_recv, g_send, g_recv, t_send, t_recv,
    p_send, p_recv, c_send, c_recv, l_send, l_recv, m_send, m_recv,
    b_send, b_recv, bx_send, bx_recv, e_send, e_recv, ex_send, ex_recv, u_send, u_recv, ur_send, in_sem, down_sem, up_sem, met_sem, dp_sem,
):
    n = C * D
    count = x_ref.shape[1]
    rows = freqs // n
    hd = HEAD_DIM
    first = part.shape[1]
    seg = lax.axis_index("segment")
    ctx = lax.axis_index("ctx")
    dp = lax.axis_index("dp")
    me = ctx * D + dp
    after = {"segment": lax.rem(seg + 1, S)}
    before = {"segment": lax.rem(seg + S - 1, S)}
    most = direct.shape[0] - 1
    early = heads - most
    def gives(at):
        reach = jnp.where(dp == D - 1, 1, jnp.where(dp == D - 3, FAR, 0))
        return at < reach

    give = gives(seg)
    take = jnp.logical_and(seg > 0, gives(seg - 1))
    mine = early - jnp.where(give, 1, 0)
    swap = jnp.logical_and(dp == D - 2, C == 2)
    host = jnp.logical_and(swap, ctx == 0)
    guest = jnp.logical_and(swap, ctx == 1)
    low = jnp.where(swap, 1, 0)
    peers = []
    for r in range(1, n):
        p = lax.rem(me + r, n)
        peers.append({"ctx": p // D, "dp": lax.rem(p, D)})
    ring = [{"ctx": lax.rem(ctx + r, C)} for r in range(1, C)]
    clips = [{"dp": lax.rem(dp + r, D)} for r in range(1, D)]

    def cols(h):
        return pl.ds(pl.multiple_of(h * hd, hd), hd)

    def tell(sem, who):
        pl.semaphore_signal(sem, inc=1, device_id=who, device_id_type=MESH)

    barrier = pltpu.get_barrier_semaphore()
    for who in ring:
        tell(barrier, who)

    pairs = D == 4
    if pairs:
        @pl.when(dp < 2)
        def _():
            tell(barrier, {"dp": dp + 2})

        @pl.when(lax.rem(dp, 2) == 1)
        def _():
            tell(barrier, {"dp": dp - 1})

        met = jnp.where(dp >= 2, 1, 0) + jnp.where(lax.rem(dp, 2) == 0, 1, 0)
    else:
        @pl.loop(dp + 1, D)
        def _(d):
            tell(barrier, {"dp": d})

        met = dp

    @pl.when(seg < S - 1)
    def _():
        tell(barrier, after)

    loads = [
        pltpu.make_async_copy(pos_ref, posv, load_sem.at[0]),
        pltpu.make_async_copy(x_ref.at[1], xv.at[1], load_sem.at[1]),
        pltpu.make_async_copy(x_ref.at[0], xv.at[0], load_sem.at[2]),
        pltpu.make_async_copy(w_ref, wv, load_sem.at[3]),
        pltpu.make_async_copy(cot_ref, cotv, load_sem.at[4]),
    ]

    pl.semaphore_wait(barrier, C - 1 + met + jnp.where(seg > 0, 1, 0))

    def send_values(h):
        for r in range(1, C):
            pltpu.make_async_remote_copy(
                src_ref=x_ref.at[2, :, cols(h)],
                dst_ref=kv.at[h, 1, pl.ds(r * count, count), :],
                send_sem=kv_send, recv_sem=kv_recv.at[h],
                device_id=ring[r - 1], device_id_type=MESH,
            ).start()

    def send_keys(h):
        for r in range(1, C):
            pltpu.make_async_remote_copy(
                src_ref=kv.at[h, 0, pl.ds(0, count), :],
                dst_ref=kv.at[h, 0, pl.ds(r * count, count), :],
                send_sem=kv_send, recv_sem=kv_recv.at[h],
                device_id=ring[r - 1], device_id_type=MESH,
            ).start()

    lead = min(LEAD, early - 2)

    @pl.loop(low, low + lead)
    def _(h):
        send_values(h)

    if pairs:
        @pl.when(dp == 2)
        def _():
            tell(dp_sem, {"dp": dp - 2})
            tell(dp_sem, {"dp": dp + 1})
    else:
        @pl.loop(0, dp)
        def _(d):
            tell(dp_sem, {"dp": d})

    for load in loads[:3]:
        load.start()

    @pl.loop(0, heads)
    def _(h):
        pltpu.make_async_copy(x_ref.at[2, :, cols(h)], kv.at[h, 1, pl.ds(0, count), :], v_sem).start()


    gain_copy = pltpu.make_async_remote_copy(
        src_ref=gain_ref, dst_ref=gains, send_sem=g_send, recv_sem=g_recv,
        device_id=before, device_id_type=MESH,
    )

    @pl.when(seg > 0)
    def _():
        tell(in_sem, before)
        gain_copy.start()

    @pl.when(seg < S - 1)
    def _():
        pl.semaphore_wait(in_sem, 1)

    @pl.when(seg == S - 2)
    def _():
        tell(down_sem, before)

    @pl.when(seg == 1)
    def _():
        tell(up_sem, after)

    @pl.when(seg < S - 2)
    def _():
        pl.semaphore_wait(down_sem, 1)

        @pl.when(seg > 0)
        def _():
            tell(down_sem, before)

    @pl.when(seg == 0)
    def _():
        gain_copy.start()

    @pl.when(seg > 1)
    def _():
        pl.semaphore_wait(up_sem, 1)

        @pl.when(seg < S - 1)
        def _():
            tell(up_sem, after)

    if pairs:
        pl.semaphore_wait(dp_sem, 1)

        @pl.when(dp == 0)
        def _():
            tell(dp_sem, {"dp": dp + 1})
            tell(dp_sem, {"dp": dp + 2})
    else:
        @pl.when(dp < D - 1)
        def _():
            pl.semaphore_wait(dp_sem, D - 1 - dp)

    for who in ring:
        tell(met_sem, who)
    own = kv.at[:, 1, pl.ds(0, count), :]
    pltpu.make_async_copy(own, own, v_sem).wait()

    for load in loads[3:]:
        load.start()

    def hand_over(source, which, h, send=b_send, recv=b_recv):
        pltpu.make_async_remote_copy(
            src_ref=source, dst_ref=direct.at[heads - 1 - h, which, pl.ds(0, count), :],
            send_sem=send, recv_sem=recv, device_id=after, device_id_type=MESH,
        ).start()

    @pl.loop(early, heads)
    def _(h):
        hand_over(kv.at[h, 1, pl.ds(0, count), :], 1, h)

    loads[0].wait()
    pos = jnp.transpose(jnp.broadcast_to(posv[...], (hd, count)))
    s, c = sincos(rope_angles(pos))
    lane = lax.broadcasted_iota(jnp.int32, (count, hd), 1)
    cosv[...] = c
    sinv[...] = jnp.where(lane < hd // 2, -s, s)

    tbuf[0] = jnp.full((8, hd), t_ref[0, 0].astype(jnp.float32), jnp.float32)
    for r in range(1, D):
        pltpu.make_async_remote_copy(
            src_ref=tbuf.at[0], dst_ref=tbuf.at[r], send_sem=t_send, recv_sem=t_recv,
            device_id=clips[r - 1], device_id_type=MESH,
        ).start()

    def inverse_norm(which):
        def add(h, acc):
            x = xv[which, :, cols(h)].astype(jnp.float32)
            return acc + x * x

        acc = lax.fori_loop(0, heads, add, jnp.zeros((count, hd), jnp.float32))
        mean = jnp.sum(acc, axis=1, keepdims=True) / (heads * hd)
        return lax.rsqrt(mean + 1e-06)

    def turned(which, h, inv):
        x = xv[which, :, cols(h)].astype(jnp.float32)
        x = x * inv * gains[which : which + 1, cols(h)]
        return (x * cosv[...] + pltpu.roll(x, hd // 2, 1) * sinv[...]).astype(jnp.bfloat16)

    loads[1].wait()
    inv_k = inverse_norm(1)
    loads[2].wait()
    inv_q = inverse_norm(0)
    gain_copy.wait_recv()

    def forward(slot, sems, send=bx_send):
        for which in range(2):
            for r in range(1, C):
                pltpu.make_async_remote_copy(
                    src_ref=direct.at[slot, which, pl.ds(0, count), :],
                    dst_ref=direct.at[slot, which, pl.ds(r * count, count), :],
                    send_sem=send, recv_sem=sems[which],
                    device_id=ring[r - 1], device_id_type=MESH,
                ).start()

    @pl.when(swap)
    def _():
        kv[0, 0, 0:count, :] = turned(1, 0, inv_k)
        qbuf[0] = turned(0, 0, inv_q)

    @pl.when(guest)
    def _():
        for i, source in enumerate((kv.at[0, 0, pl.ds(0, count), :], kv.at[0, 1, pl.ds(0, count), :], qbuf.at[0])):
            pltpu.make_async_remote_copy(
                src_ref=source, dst_ref=ubuf.at[i], send_sem=u_send, recv_sem=u_recv,
                device_id=ring[0], device_id_type=MESH,
            ).start()

    @pl.loop(low, mine)
    def _(h):
        kv[h, 0, 0:count, :] = turned(1, h, inv_k)
        send_keys(h)

        @pl.when(h + lead < mine)
        def _():
            send_values(h + lead)

    @pl.loop(early, heads)
    def _(h):
        kv[h, 0, 0:count, :] = turned(1, h, inv_k)
        qbuf[h] = turned(0, h, inv_q)
        hand_over(kv.at[h, 0, pl.ds(0, count), :], 0, h)
        hand_over(qbuf.at[h], 2, h)

    spare = early - 1

    @pl.when(give)
    def _():
        kv[spare, 0, 0:count, :] = turned(1, spare, inv_k)
        qbuf[spare] = turned(0, spare, inv_q)
        hand_over(kv.at[spare, 1, pl.ds(0, count), :], 1, spare, e_send, e_recv)
        hand_over(kv.at[spare, 0, pl.ds(0, count), :], 0, spare, e_send, e_recv)
        hand_over(qbuf.at[spare], 2, spare, e_send, e_recv)

    @pl.loop(low, mine)
    def _(h):
        qbuf[h] = turned(0, h, inv_q)

    half = freqs // 2
    decay = -math.log(10000.0) / half
    index = lax.broadcasted_iota(jnp.int32, (half, hd), 0).astype(jnp.float32)
    es, ec = sincos(tbuf[0, 0:1, :] * jnp.exp(index * decay))
    loads[3].wait()

    @pl.loop(0, heads)
    def _(h):
        terms = wv[0:half, cols(h)] * ec + wv[half:freqs, cols(h)] * es
        gate[pl.ds(h, 1), :] = jnp.sum(terms, axis=0, keepdims=True)

    if D > 1:
        others = tbuf.at[pl.ds(1, D - 1)]
        pltpu.make_async_copy(others, others, t_recv).wait()
    at = lax.broadcasted_iota(jnp.int32, (rows, hd), 0) + me * rows
    freq = jnp.exp((at % half).astype(jnp.float32) * decay)
    for j in range(D):
        s, c = sincos(tbuf[j, 0:1, :] * freq)
        emb[j] = jnp.where(at < half, c, s)
    loads[4].wait()

    scale = 1.0 / hd**0.5

    def weigh(queries, keys):
        scores = lax.dot_general(
            queries, keys, (((1,), (1,)), ((), ())), preferred_element_type=jnp.float32
        ) * scale
        expo = jnp.exp(scores - jnp.max(scores, axis=1, keepdims=True))
        return expo.astype(jnp.bfloat16), jnp.sum(expo, axis=1, keepdims=True)

    def attend(h):
        arrived = kv.at[h, :, pl.ds(count, (C - 1) * count), :]
        pltpu.make_async_copy(arrived, arrived, kv_recv.at[h]).wait()
        weights, norm = weigh(qbuf[h], kv[h, 0])
        mixed = jnp.dot(weights, kv[h, 1], preferred_element_type=jnp.float32)
        abuf[h] = (mixed / norm).astype(jnp.bfloat16)
        pltpu.make_async_remote_copy(
            src_ref=abuf.at[h], dst_ref=rbuf.at[h], send_sem=a_send, recv_sem=a_recv.at[h // GROUP],
            device_id=after, device_id_type=MESH,
        ).start()

    def use(h, attn):
        out_ref[:, cols(h)] = (attn * gate[pl.ds(h, 1), :]).astype(jnp.bfloat16)
        cot = cotv[:, cols(h)].astype(jnp.float32)
        return jnp.sum(attn * cot, axis=0, keepdims=True)

    def finish(g):
        some = rbuf.at[pl.ds(g * GROUP, GROUP)]
        pltpu.make_async_copy(some, some, a_recv.at[g]).wait()
        for i in range(GROUP):
            h = g * GROUP + i
            part[0, pl.ds(h, 1), :] = use(h, rbuf[h].astype(jnp.float32))

    @pl.when(host)
    def _():
        some = ubuf.at[pl.ds(0, 3)]
        pltpu.make_async_copy(some, some, u_recv).wait()
        kv[0, 0, count : 2 * count, :] = ubuf[0]
        kv[0, 1, count : 2 * count, :] = ubuf[1]
        ubuf[3] = qbuf[0]

        @pl.loop(0, 2)
        def _(i):
            weights, norm = weigh(ubuf[2 + i], kv[0, 0])
            mixed = jnp.dot(weights, kv[0, 1], preferred_element_type=jnp.float32)
            ures[i] = (mixed / norm).astype(jnp.bfloat16)
            pltpu.make_async_remote_copy(
                src_ref=ures.at[i], dst_ref=rbuf.at[0], send_sem=ur_send, recv_sem=a_recv.at[0],
                device_id={"segment": after["segment"], "ctx": 1 - i}, device_id_type=MESH,
            ).start()

    @pl.loop(low, mine)
    def _(h):
        attend(h)

        @pl.when(h == FORWARD_AT)
        def _():
            here = direct.at[pl.ds(0, most), :, pl.ds(0, count), :]
            pltpu.make_async_copy(here, here, b_recv).wait()

            @pl.when(take)
            def _():
                more = direct.at[most, :, pl.ds(0, count), :]
                pltpu.make_async_copy(more, more, e_recv).wait()
                forward(most, (ex_recv, ex_recv), ex_send)

            @pl.loop(early, heads - 1)
            def _(g):
                slot = heads - 1 - g
                forward(slot, (bx_recv.at[slot - 1], bx_recv.at[slot - 1]))

        @pl.when(jnp.logical_and(lax.rem(h, GROUP) == GROUP - 1, h >= LAG * GROUP))
        def _():
            finish(h // GROUP - LAG)

    groups = early // GROUP

    @pl.loop(mine // GROUP - LAG, first // GROUP)
    def _(g):
        finish(g)

    for r in range(1, C):
        pltpu.make_async_remote_copy(
            src_ref=part.at[0], dst_ref=part.at[r], send_sem=p_send, recv_sem=p_recv,
            device_id=ring[r - 1], device_id_type=MESH,
        ).start()

    forward(0, (bx_recv.at[most - 1], bx_recv.at[most]))

    def direct_head(h, sem):
        slot = heads - 1 - h
        arrived = direct.at[slot, pl.ds(0, 2), pl.ds(count, (C - 1) * count), :]
        pltpu.make_async_copy(arrived, arrived, sem).wait()
        weights, norm = weigh(direct[slot, 2, 0:count, :], direct[slot, 0])
        mixed = jnp.dot(weights, direct[slot, 1], preferred_element_type=jnp.float32)
        late[0, pl.ds(h - first, 1), :] = use(h, mixed / norm)

    @pl.when(take)
    def _():
        direct_head(spare, ex_recv)

    @pl.loop(early, heads - 2)
    def _(h):
        direct_head(h, bx_recv.at[heads - 2 - h])

    if C > 1:
        others = part.at[pl.ds(1, C - 1)]
        pltpu.make_async_copy(others, others, p_recv).wait()
    acc = part[0]
    for r in range(1, C):
        acc = acc + part[r]
    total[0] = acc
    for r in range(1, D):
        pltpu.make_async_remote_copy(
            src_ref=total.at[0], dst_ref=total.at[r], send_sem=c_send, recv_sem=c_recv,
            device_id=clips[r - 1], device_id_type=MESH,
        ).start()

    direct_head(heads - 2, bx_recv.at[0])

    def results(g, size):
        some = rbuf.at[pl.ds(g * GROUP, size)]
        pltpu.make_async_copy(some, some, a_recv.at[g]).wait()
        for i in range(size):
            h = g * GROUP + i
            late[0, pl.ds(h - first, 1), :] = use(h, rbuf[h].astype(jnp.float32))

    @pl.loop(first // GROUP, groups - 1)
    def _(g):
        results(g, GROUP)

    @pl.when(take)
    def _():
        results(groups - 1, GROUP - 1)

    @pl.when(jnp.logical_not(take))
    def _():
        results(groups - 1, GROUP)

    pl.semaphore_wait(met_sem, C - 1)
    order = sorted(range(1, n), key=lambda r: (r % D == 0) + (r < D or r > n - D))

    def share(rows_of, send, recv):
        for r in order:
            pltpu.make_async_remote_copy(
                src_ref=rows_of.at[0], dst_ref=rows_of.at[r], send_sem=send, recv_sem=recv,
                device_id=peers[r - 1], device_id_type=MESH,
            ).start()

    share(late, l_send, l_recv)
    final = slice((heads - 1) * hd, heads * hd)
    arrived = direct.at[0, 0, pl.ds(count, (C - 1) * count), :]
    pltpu.make_async_copy(arrived, arrived, bx_recv.at[most - 1]).wait()
    weights, norm = weigh(direct[0, 2, 0:count, :], direct[0, 0])
    inverse = 1.0 / norm
    cot = cotv[:, final].astype(jnp.float32) * inverse
    arrived = direct.at[0, 1, pl.ds(count, (C - 1) * count), :]
    pltpu.make_async_copy(arrived, arrived, bx_recv.at[most]).wait()
    mixed = jnp.dot(weights, direct[0, 1], preferred_element_type=jnp.float32)
    last[0] = jnp.sum(mixed * cot, axis=0, keepdims=True)
    share(last, m_send, m_recv)
    out_ref[:, final] = (mixed * inverse * gate[heads - 1 : heads, :]).astype(jnp.bfloat16)


    gain_copy.wait_send()
    if D > 1:
        others = tbuf.at[pl.ds(1, D - 1)]
        pltpu.make_async_copy(others, others, t_send).wait()
        others = total.at[pl.ds(1, D - 1)]
        pltpu.make_async_copy(others, others, c_recv).wait()
        pltpu.make_async_copy(others, others, c_send).wait()
    if C > 1:
        others = part.at[pl.ds(1, C - 1)]
        pltpu.make_async_copy(others, others, p_send).wait()

    @pl.loop(0, first)
    def _(h):
        acc = emb[0] * total[0, pl.ds(h, 1), :]
        for j in range(1, D):
            acc = acc + emb[j] * total[j, pl.ds(h, 1), :]
        grad_ref[:, cols(h)] = acc

    def drain(number):
        sent = kv.at[pl.ds(0, number), :, pl.ds(count, (C - 1) * count), :]
        pltpu.make_async_copy(sent, sent, kv_send).wait()
        sent = abuf.at[pl.ds(0, number)]
        pltpu.make_async_copy(sent, sent, a_send).wait()

    fewer = jnp.logical_or(give, swap)

    @pl.when(fewer)
    def _():
        drain(early - 1)

    @pl.when(jnp.logical_not(fewer))
    def _():
        drain(early)

    @pl.when(give)
    def _():
        sent = direct.at[most, :, pl.ds(0, count), :]
        pltpu.make_async_copy(sent, sent, e_send).wait()

    @pl.when(guest)
    def _():
        sent = ubuf.at[pl.ds(0, 3)]
        pltpu.make_async_copy(sent, sent, u_send).wait()

    @pl.when(host)
    def _():
        pltpu.make_async_copy(ures, ures, ur_send).wait()

    @pl.when(take)
    def _():
        sent = direct.at[most, pl.ds(0, 2), pl.ds(count, (C - 1) * count), :]
        pltpu.make_async_copy(sent, sent, ex_send).wait()

    sent = direct.at[pl.ds(0, most), :, pl.ds(0, count), :]
    pltpu.make_async_copy(sent, sent, b_send).wait()
    sent = direct.at[pl.ds(0, most), pl.ds(0, 2), pl.ds(count, (C - 1) * count), :]
    pltpu.make_async_copy(sent, sent, bx_send).wait()

    def grads(rows_of, recv, send, start):
        others = rows_of.at[pl.ds(1, n - 1)]
        pltpu.make_async_copy(others, others, recv).wait()
        sums = []
        for j in range(D):
            acc = rows_of[j]
            for c in range(1, C):
                acc = acc + rows_of[j + c * D]
            sums.append(acc)
        for i in range(rows_of.shape[1]):
            acc = emb[0] * sums[0][i : i + 1, :]
            for j in range(1, D):
                acc = acc + emb[j] * sums[j][i : i + 1, :]
            grad_ref[:, (start + i) * hd : (start + i + 1) * hd] = acc
        pltpu.make_async_copy(others, others, send).wait()

    grads(late, l_recv, l_send, first)
    grads(last, m_recv, m_send, heads - 1)


def store(attn_ref, grad_ref, out_ref, grads_ref, out_sem, grad_sem):
    copies = [
        pltpu.make_async_copy(attn_ref, out_ref, out_sem),
        pltpu.make_async_copy(grad_ref, grads_ref, grad_sem),
    ]
    for copy in copies:
        copy.start()
    for copy in copies:
        copy.wait()


def local(S, C, D, qkv, qk_gain, mod_weight, positions, timesteps, cotangent):
    count, _, width = qkv.shape[2:]
    freqs = mod_weight.shape[1]
    heads = width // HEAD_DIM
    n = C * D
    rows = freqs // n
    hd = HEAD_DIM
    most = DIRECT
    early = heads - most
    first = FIRST
    if S < 3 or C < 2 or D < 2 or early % GROUP or first % GROUP or first + GROUP > early or FORWARD_AT >= early:
        raise ValueError("unsupported mesh")
    bf, f32 = jnp.bfloat16, jnp.float32
    vmem = pl.BlockSpec(memory_space=pltpu.VMEM)
    hbm = pl.BlockSpec(memory_space=pltpu.HBM)
    dma = pltpu.SemaphoreType.DMA
    regular = pltpu.SemaphoreType.REGULAR
    pin = functools.partial(pltpu.with_memory_space_constraint, memory_space=pltpu.HBM)
    attn, grad = pl.pallas_call(
        functools.partial(body, S, C, D, heads, freqs),
        out_shape=(
            jax.ShapeDtypeStruct((count, width), bf),
            jax.ShapeDtypeStruct((rows, width), f32),
        ),
        in_specs=[hbm] * 4 + [pl.BlockSpec(memory_space=pltpu.SMEM), hbm],
        out_specs=(vmem, vmem),
        scratch_shapes=[
            pltpu.VMEM((2, count, width), bf),
            pltpu.VMEM((freqs, width), f32),
            pltpu.VMEM((count, width), bf),
            pltpu.VMEM((heads, 2, C * count, hd), bf),
            pltpu.VMEM((heads, count, hd), bf),
            pltpu.VMEM((heads, count, hd), bf),
            pltpu.VMEM((heads, count, hd), bf),
            pltpu.VMEM((most + 1, 3, C * count, hd), bf),
            pltpu.VMEM((2, width), f32),
            pltpu.VMEM((1, count), jnp.int32),
            pltpu.VMEM((D, 8, hd), f32),
            pltpu.VMEM((-(-heads // 8) * 8, hd), f32),
            pltpu.VMEM((D, rows, hd), f32),
            pltpu.VMEM((count, hd), f32),
            pltpu.VMEM((count, hd), f32),
            pltpu.VMEM((C, first, hd), f32),
            pltpu.VMEM((D, first, hd), f32),
            pltpu.VMEM((n, heads - 1 - first, hd), f32),
            pltpu.VMEM((n, 1, hd), f32),
            pltpu.VMEM((4, count, hd), bf),
            pltpu.VMEM((2, count, hd), bf),
            dma((5,)), dma,
            dma, dma((early,)), dma, dma((early // GROUP,)),
            dma, dma, dma, dma, dma, dma, dma, dma, dma, dma, dma, dma,
            dma, dma, dma, dma((most + 1,)), dma, dma, dma, dma, dma, dma, dma,
            regular, regular, regular, regular, regular,
        ],
        compiler_params=pltpu.CompilerParams(
            collective_id=0, has_side_effects=True, vmem_limit_bytes=VMEM_LIMIT if C <= 2 else 60 << 20
        ),
    )(
        pin(jnp.moveaxis(qkv[0, 0], 1, 0)),
        pin(qk_gain[0]),
        pin(mod_weight[0]),
        pin(positions),
        timesteps,
        pin(cotangent[0, 0]),
    )
    anywhere = pl.BlockSpec(memory_space=pl.ANY)
    attn_out, gate_grad = pl.pallas_call(
        store,
        out_shape=(
            jax.ShapeDtypeStruct((count, width), bf),
            jax.ShapeDtypeStruct((rows, width), f32),
        ),
        in_specs=[anywhere, anywhere],
        out_specs=(anywhere, anywhere),
        scratch_shapes=[dma, dma],
        compiler_params=pltpu.CompilerParams(vmem_limit_bytes=4 << 20),
    )(attn, grad)
    return attn_out[None, None], gate_grad[None]


def solution(mesh):
    sizes = mesh.shape
    return jax.shard_map(
        functools.partial(local, sizes["segment"], sizes["ctx"], sizes["dp"]),
        mesh=mesh,
        in_specs=(
            P("segment", "dp", "ctx", None, None),
            P("segment", None, None),
            P("segment", None, None),
            P("dp", "ctx"),
            P("segment", "dp"),
            P("segment", "dp", "ctx", None),
        ),
        out_specs=(P("segment", "dp", "ctx", None), P("segment", ("ctx", "dp"), None)),
        check_vma=False,
    )
```

```python
import functools
import math

import jax
import jax.numpy as jnp
from jax import lax
from jax.experimental import pallas as pl
from jax.experimental.pallas import tpu as pltpu
from jax.sharding import PartitionSpec as P

HEAD_DIM = 128
GRID_ROWS = 45
GRID_COLS = 80
MESH = pl.DeviceIdType.MESH
LEAD = 12
GROUP = 5
LAG = 2
DIRECT = 5
FIRST = 5
FAR = 2
PAIRED = 10
FORWARD_AT = 8
VMEM_LIMIT = 24 << 20


def sincos(angle):
    turns = jnp.floor(angle * (2.0 / math.pi) + 0.5)
    quad = turns.astype(jnp.int32)
    r = angle - turns * 1.5703125
    r = r - turns * 4.837512969970703125e-4
    r = r - turns * 7.549789948768648e-8
    z = r * r
    sine = r + r * z * (-1.6666654611e-1 + z * (8.3321608736e-3 - z * 1.9515295891e-4))
    cosine = 1.0 - 0.5 * z + z * z * (
        4.166664568298827e-2 + z * (-1.388731625493765e-3 + z * 2.443315711809948e-5)
    )
    swap = (quad & 1) == 1
    s = jnp.where(swap, cosine, sine)
    c = jnp.where(swap, sine, cosine)
    s = jnp.where((quad & 2) == 2, -s, s)
    c = jnp.where(((quad + 1) & 2) == 2, -c, c)
    return s, c


def rope_angles(pos):
    count, hd = pos.shape
    half = hd // 2
    side = hd // 6
    first = half - 2 * side
    pair = lax.broadcasted_iota(jnp.int32, (8, hd), 1) % half
    group = jnp.where(pair < first, 0, jnp.where(pair < first + side, 1, 2))
    offset = jnp.where(group == 0, 0, jnp.where(group == 1, first, first + side))
    pairs_in = jnp.where(group == 0, first, side).astype(jnp.float32)
    freq = jnp.exp((pair - offset).astype(jnp.float32) / pairs_in * -math.log(10000.0))[0:1]
    group = group[0:1]
    frame = (pos // (GRID_ROWS * GRID_COLS)).astype(jnp.float32)
    row = (pos // GRID_COLS % GRID_ROWS).astype(jnp.float32)
    col = (pos % GRID_COLS).astype(jnp.float32)
    return jnp.where(group == 0, frame, jnp.where(group == 1, row, col)) * freq


def body(
    S, C, D, heads, freqs,
    x_ref, gain_ref, w_ref, pos_ref, t_ref, cot_ref,
    out_ref, grad_ref,
    xv, wv, cotv, kv, qbuf, abuf, rbuf, direct, gains, posv, tbuf, gate, emb, cosv, sinv,
    part, total, late, last, ubuf, ures,
    load_sem, v_sem, kv_send, kv_recv, a_send, a_recv, g_send, g_recv, t_send, t_recv,
    p_send, p_recv, c_send, c_recv, l_send, l_recv, m_send, m_recv,
    b_send, b_recv, bx_send, bx_recv, e_send, e_recv, ex_send, ex_recv, u_send, u_recv, ur_send, in_sem, down_sem, up_sem, met_sem, dp_sem,
):
    n = C * D
    count = x_ref.shape[1]
    rows = freqs // n
    hd = HEAD_DIM
    first = part.shape[1]
    seg = lax.axis_index("segment")
    ctx = lax.axis_index("ctx")
    dp = lax.axis_index("dp")
    me = ctx * D + dp
    after = {"segment": lax.rem(seg + 1, S)}
    before = {"segment": lax.rem(seg + S - 1, S)}
    most = direct.shape[0] - 1
    early = heads - most
    def gives(at):
        reach = jnp.where(dp == D - 1, 1, jnp.where(dp == D - 3, FAR, 0))
        return at < reach

    give = gives(seg)
    take = jnp.logical_and(seg > 0, gives(seg - 1))
    mine = early - jnp.where(give, 1, 0)
    swap = jnp.logical_and(dp == D - 2, C == 2)
    host = jnp.logical_and(swap, ctx == 0)
    guest = jnp.logical_and(swap, ctx == 1)
    low = jnp.where(swap, 1, 0)
    peers = []
    for r in range(1, n):
        p = lax.rem(me + r, n)
        peers.append({"ctx": p // D, "dp": lax.rem(p, D)})
    ring = [{"ctx": lax.rem(ctx + r, C)} for r in range(1, C)]
    clips = [{"dp": lax.rem(dp + r, D)} for r in range(1, D)]

    def cols(h):
        return pl.ds(pl.multiple_of(h * hd, hd), hd)

    def tell(sem, who):
        pl.semaphore_signal(sem, inc=1, device_id=who, device_id_type=MESH)

    barrier = pltpu.get_barrier_semaphore()
    for who in ring:
        tell(barrier, who)

    pairs = D == 4
    if pairs:
        @pl.when(dp < 2)
        def _():
            tell(barrier, {"dp": dp + 2})

        @pl.when(lax.rem(dp, 2) == 1)
        def _():
            tell(barrier, {"dp": dp - 1})

        met = jnp.where(dp >= 2, 1, 0) + jnp.where(lax.rem(dp, 2) == 0, 1, 0)
    else:
        @pl.loop(dp + 1, D)
        def _(d):
            tell(barrier, {"dp": d})

        met = dp

    @pl.when(seg < S - 1)
    def _():
        tell(barrier, after)

    loads = [
        pltpu.make_async_copy(pos_ref, posv, load_sem.at[0]),
        pltpu.make_async_copy(x_ref.at[1], xv.at[1], load_sem.at[1]),
        pltpu.make_async_copy(x_ref.at[0], xv.at[0], load_sem.at[2]),
        pltpu.make_async_copy(w_ref, wv, load_sem.at[3]),
        pltpu.make_async_copy(cot_ref, cotv, load_sem.at[4]),
    ]

    pl.semaphore_wait(barrier, C - 1 + met + jnp.where(seg > 0, 1, 0))

    solo = PAIRED + 1

    def spot(h):
        return jnp.minimum(h + 1, PAIRED + 2) // 2 + jnp.maximum(h - solo, 0)

    def send_values(h):
        for r in range(1, C):
            pltpu.make_async_remote_copy(
                src_ref=x_ref.at[2, :, cols(h)],
                dst_ref=kv.at[h, 1, pl.ds(r * count, count), :],
                send_sem=kv_send, recv_sem=kv_recv.at[spot(h)],
                device_id=ring[r - 1], device_id_type=MESH,
            ).start()

    def send_keys(h):
        for r in range(1, C):
            pltpu.make_async_remote_copy(
                src_ref=kv.at[h, 0, pl.ds(0, count), :],
                dst_ref=kv.at[h, 0, pl.ds(r * count, count), :],
                send_sem=kv_send, recv_sem=kv_recv.at[spot(h)],
                device_id=ring[r - 1], device_id_type=MESH,
            ).start()

    lead = min(LEAD, early - 2)

    @pl.loop(low, low + lead)
    def _(h):
        send_values(h)

    if pairs:
        @pl.when(dp == 2)
        def _():
            tell(dp_sem, {"dp": dp - 2})
            tell(dp_sem, {"dp": dp + 1})
    else:
        @pl.loop(0, dp)
        def _(d):
            tell(dp_sem, {"dp": d})

    for load in loads[:3]:
        load.start()

    @pl.loop(0, heads)
    def _(h):
        pltpu.make_async_copy(x_ref.at[2, :, cols(h)], kv.at[h, 1, pl.ds(0, count), :], v_sem).start()


    gain_copy = pltpu.make_async_remote_copy(
        src_ref=gain_ref, dst_ref=gains, send_sem=g_send, recv_sem=g_recv,
        device_id=before, device_id_type=MESH,
    )

    @pl.when(seg > 0)
    def _():
        tell(in_sem, before)
        gain_copy.start()

    @pl.when(seg < S - 1)
    def _():
        pl.semaphore_wait(in_sem, 1)

    @pl.when(seg == S - 2)
    def _():
        tell(down_sem, before)

    @pl.when(seg == 1)
    def _():
        tell(up_sem, after)

    @pl.when(seg < S - 2)
    def _():
        pl.semaphore_wait(down_sem, 1)

        @pl.when(seg > 0)
        def _():
            tell(down_sem, before)

    @pl.when(seg == 0)
    def _():
        gain_copy.start()

    @pl.when(seg > 1)
    def _():
        pl.semaphore_wait(up_sem, 1)

        @pl.when(seg < S - 1)
        def _():
            tell(up_sem, after)

    if pairs:
        pl.semaphore_wait(dp_sem, 1)

        @pl.when(dp == 0)
        def _():
            tell(dp_sem, {"dp": dp + 1})
            tell(dp_sem, {"dp": dp + 2})
    else:
        @pl.when(dp < D - 1)
        def _():
            pl.semaphore_wait(dp_sem, D - 1 - dp)

    for who in ring:
        tell(met_sem, who)
    own = kv.at[:, 1, pl.ds(0, count), :]
    pltpu.make_async_copy(own, own, v_sem).wait()

    for load in loads[3:]:
        load.start()

    def hand_over(source, which, h, send=b_send, recv=b_recv):
        pltpu.make_async_remote_copy(
            src_ref=source, dst_ref=direct.at[heads - 1 - h, which, pl.ds(0, count), :],
            send_sem=send, recv_sem=recv, device_id=after, device_id_type=MESH,
        ).start()

    @pl.loop(early, heads)
    def _(h):
        hand_over(kv.at[h, 1, pl.ds(0, count), :], 1, h)

    loads[0].wait()
    pos = jnp.transpose(jnp.broadcast_to(posv[...], (hd, count)))
    s, c = sincos(rope_angles(pos))
    lane = lax.broadcasted_iota(jnp.int32, (count, hd), 1)
    cosv[...] = c
    sinv[...] = jnp.where(lane < hd // 2, -s, s)

    tbuf[0] = jnp.full((8, hd), t_ref[0, 0].astype(jnp.float32), jnp.float32)
    for r in range(1, D):
        pltpu.make_async_remote_copy(
            src_ref=tbuf.at[0], dst_ref=tbuf.at[r], send_sem=t_send, recv_sem=t_recv,
            device_id=clips[r - 1], device_id_type=MESH,
        ).start()

    def inverse_norm(which):
        def add(h, acc):
            x = xv[which, :, cols(h)].astype(jnp.float32)
            return acc + x * x

        acc = lax.fori_loop(0, heads, add, jnp.zeros((count, hd), jnp.float32))
        mean = jnp.sum(acc, axis=1, keepdims=True) / (heads * hd)
        return lax.rsqrt(mean + 1e-06)

    def turned(which, h, inv):
        x = xv[which, :, cols(h)].astype(jnp.float32)
        x = x * inv * gains[which : which + 1, cols(h)]
        return (x * cosv[...] + pltpu.roll(x, hd // 2, 1) * sinv[...]).astype(jnp.bfloat16)

    loads[1].wait()
    inv_k = inverse_norm(1)
    loads[2].wait()
    inv_q = inverse_norm(0)
    gain_copy.wait_recv()

    def forward(slot, sems, send=bx_send):
        for which in range(2):
            for r in range(1, C):
                pltpu.make_async_remote_copy(
                    src_ref=direct.at[slot, which, pl.ds(0, count), :],
                    dst_ref=direct.at[slot, which, pl.ds(r * count, count), :],
                    send_sem=send, recv_sem=sems[which],
                    device_id=ring[r - 1], device_id_type=MESH,
                ).start()

    @pl.when(swap)
    def _():
        kv[0, 0, 0:count, :] = turned(1, 0, inv_k)
        qbuf[0] = turned(0, 0, inv_q)

    @pl.when(guest)
    def _():
        for i, source in enumerate((kv.at[0, 0, pl.ds(0, count), :], kv.at[0, 1, pl.ds(0, count), :], qbuf.at[0])):
            pltpu.make_async_remote_copy(
                src_ref=source, dst_ref=ubuf.at[i], send_sem=u_send, recv_sem=u_recv,
                device_id=ring[0], device_id_type=MESH,
            ).start()

    @pl.loop(low, mine)
    def _(h):
        kv[h, 0, 0:count, :] = turned(1, h, inv_k)
        send_keys(h)

        @pl.when(h + lead < mine)
        def _():
            send_values(h + lead)

    @pl.loop(early, heads)
    def _(h):
        kv[h, 0, 0:count, :] = turned(1, h, inv_k)
        qbuf[h] = turned(0, h, inv_q)
        hand_over(kv.at[h, 0, pl.ds(0, count), :], 0, h)
        hand_over(qbuf.at[h], 2, h)

    spare = early - 1

    @pl.when(give)
    def _():
        kv[spare, 0, 0:count, :] = turned(1, spare, inv_k)
        qbuf[spare] = turned(0, spare, inv_q)
        hand_over(kv.at[spare, 1, pl.ds(0, count), :], 1, spare, e_send, e_recv)
        hand_over(kv.at[spare, 0, pl.ds(0, count), :], 0, spare, e_send, e_recv)
        hand_over(qbuf.at[spare], 2, spare, e_send, e_recv)

    @pl.loop(low, mine)
    def _(h):
        qbuf[h] = turned(0, h, inv_q)

    half = freqs // 2
    decay = -math.log(10000.0) / half
    index = lax.broadcasted_iota(jnp.int32, (half, hd), 0).astype(jnp.float32)
    es, ec = sincos(tbuf[0, 0:1, :] * jnp.exp(index * decay))
    loads[3].wait()

    @pl.loop(0, heads)
    def _(h):
        terms = wv[0:half, cols(h)] * ec + wv[half:freqs, cols(h)] * es
        gate[pl.ds(h, 1), :] = jnp.sum(terms, axis=0, keepdims=True)

    if D > 1:
        others = tbuf.at[pl.ds(1, D - 1)]
        pltpu.make_async_copy(others, others, t_recv).wait()
    at = lax.broadcasted_iota(jnp.int32, (rows, hd), 0) + me * rows
    freq = jnp.exp((at % half).astype(jnp.float32) * decay)
    for j in range(D):
        s, c = sincos(tbuf[j, 0:1, :] * freq)
        emb[j] = jnp.where(at < half, c, s)
    loads[4].wait()

    scale = 1.0 / hd**0.5

    def weigh(queries, keys):
        scores = lax.dot_general(
            queries, keys, (((1,), (1,)), ((), ())), preferred_element_type=jnp.float32
        ) * scale
        expo = jnp.exp(scores - jnp.max(scores, axis=1, keepdims=True))
        return expo.astype(jnp.bfloat16), jnp.sum(expo, axis=1, keepdims=True)

    def attend(h):
        @pl.when(jnp.logical_and(lax.rem(h, 2) == 1, h < solo))
        def _():
            arrived = kv.at[pl.ds(h, 2), :, pl.ds(count, (C - 1) * count), :]
            pltpu.make_async_copy(arrived, arrived, kv_recv.at[spot(h)]).wait()

        @pl.when(jnp.logical_or(h == 0, h >= solo))
        def _():
            arrived = kv.at[h, :, pl.ds(count, (C - 1) * count), :]
            pltpu.make_async_copy(arrived, arrived, kv_recv.at[spot(h)]).wait()

        weights, norm = weigh(qbuf[h], kv[h, 0])
        mixed = jnp.dot(weights, kv[h, 1], preferred_element_type=jnp.float32)
        abuf[h] = (mixed / norm).astype(jnp.bfloat16)
        pltpu.make_async_remote_copy(
            src_ref=abuf.at[h], dst_ref=rbuf.at[h], send_sem=a_send, recv_sem=a_recv.at[h // GROUP],
            device_id=after, device_id_type=MESH,
        ).start()

    def use(h, attn):
        out_ref[:, cols(h)] = (attn * gate[pl.ds(h, 1), :]).astype(jnp.bfloat16)
        cot = cotv[:, cols(h)].astype(jnp.float32)
        return jnp.sum(attn * cot, axis=0, keepdims=True)

    def finish(g):
        some = rbuf.at[pl.ds(g * GROUP, GROUP)]
        pltpu.make_async_copy(some, some, a_recv.at[g]).wait()
        for i in range(GROUP):
            h = g * GROUP + i
            part[0, pl.ds(h, 1), :] = use(h, rbuf[h].astype(jnp.float32))

    @pl.when(host)
    def _():
        some = ubuf.at[pl.ds(0, 3)]
        pltpu.make_async_copy(some, some, u_recv).wait()
        kv[0, 0, count : 2 * count, :] = ubuf[0]
        kv[0, 1, count : 2 * count, :] = ubuf[1]
        ubuf[3] = qbuf[0]

        @pl.loop(0, 2)
        def _(i):
            weights, norm = weigh(ubuf[2 + i], kv[0, 0])
            mixed = jnp.dot(weights, kv[0, 1], preferred_element_type=jnp.float32)
            ures[i] = (mixed / norm).astype(jnp.bfloat16)
            pltpu.make_async_remote_copy(
                src_ref=ures.at[i], dst_ref=rbuf.at[0], send_sem=ur_send, recv_sem=a_recv.at[0],
                device_id={"segment": after["segment"], "ctx": 1 - i}, device_id_type=MESH,
            ).start()

    @pl.loop(low, mine)
    def _(h):
        attend(h)

        @pl.when(h == FORWARD_AT)
        def _():
            here = direct.at[pl.ds(0, most), :, pl.ds(0, count), :]
            pltpu.make_async_copy(here, here, b_recv).wait()

            @pl.when(take)
            def _():
                more = direct.at[most, :, pl.ds(0, count), :]
                pltpu.make_async_copy(more, more, e_recv).wait()
                forward(most, (ex_recv, ex_recv), ex_send)

            @pl.loop(early, heads - 1)
            def _(g):
                slot = heads - 1 - g
                forward(slot, (bx_recv.at[slot - 1], bx_recv.at[slot - 1]))

        @pl.when(jnp.logical_and(lax.rem(h, GROUP) == GROUP - 1, h >= LAG * GROUP))
        def _():
            finish(h // GROUP - LAG)

    groups = early // GROUP

    @pl.loop(mine // GROUP - LAG, first // GROUP)
    def _(g):
        finish(g)

    for r in range(1, C):
        pltpu.make_async_remote_copy(
            src_ref=part.at[0], dst_ref=part.at[r], send_sem=p_send, recv_sem=p_recv,
            device_id=ring[r - 1], device_id_type=MESH,
        ).start()

    forward(0, (bx_recv.at[most - 1], bx_recv.at[most]))

    def direct_head(h, sem):
        slot = heads - 1 - h
        arrived = direct.at[slot, pl.ds(0, 2), pl.ds(count, (C - 1) * count), :]
        pltpu.make_async_copy(arrived, arrived, sem).wait()
        weights, norm = weigh(direct[slot, 2, 0:count, :], direct[slot, 0])
        mixed = jnp.dot(weights, direct[slot, 1], preferred_element_type=jnp.float32)
        late[0, pl.ds(h - first, 1), :] = use(h, mixed / norm)

    @pl.when(take)
    def _():
        direct_head(spare, ex_recv)

    @pl.loop(early, heads - 2)
    def _(h):
        direct_head(h, bx_recv.at[heads - 2 - h])

    if C > 1:
        others = part.at[pl.ds(1, C - 1)]
        pltpu.make_async_copy(others, others, p_recv).wait()
    acc = part[0]
    for r in range(1, C):
        acc = acc + part[r]
    total[0] = acc
    for r in range(1, D):
        pltpu.make_async_remote_copy(
            src_ref=total.at[0], dst_ref=total.at[r], send_sem=c_send, recv_sem=c_recv,
            device_id=clips[r - 1], device_id_type=MESH,
        ).start()

    direct_head(heads - 2, bx_recv.at[0])

    def results(g, size):
        some = rbuf.at[pl.ds(g * GROUP, size)]
        pltpu.make_async_copy(some, some, a_recv.at[g]).wait()
        for i in range(size):
            h = g * GROUP + i
            late[0, pl.ds(h - first, 1), :] = use(h, rbuf[h].astype(jnp.float32))

    @pl.loop(first // GROUP, groups - 1)
    def _(g):
        results(g, GROUP)

    @pl.when(take)
    def _():
        results(groups - 1, GROUP - 1)

    @pl.when(jnp.logical_not(take))
    def _():
        results(groups - 1, GROUP)

    pl.semaphore_wait(met_sem, C - 1)
    order = sorted(range(1, n), key=lambda r: (r % D == 0) + (r < D or r > n - D))

    def share(rows_of, send, recv):
        for r in order:
            pltpu.make_async_remote_copy(
                src_ref=rows_of.at[0], dst_ref=rows_of.at[r], send_sem=send, recv_sem=recv,
                device_id=peers[r - 1], device_id_type=MESH,
            ).start()

    share(late, l_send, l_recv)
    final = slice((heads - 1) * hd, heads * hd)
    arrived = direct.at[0, 0, pl.ds(count, (C - 1) * count), :]
    pltpu.make_async_copy(arrived, arrived, bx_recv.at[most - 1]).wait()
    weights, norm = weigh(direct[0, 2, 0:count, :], direct[0, 0])
    inverse = 1.0 / norm
    cot = cotv[:, final].astype(jnp.float32) * inverse
    arrived = direct.at[0, 1, pl.ds(count, (C - 1) * count), :]
    pltpu.make_async_copy(arrived, arrived, bx_recv.at[most]).wait()
    mixed = jnp.dot(weights, direct[0, 1], preferred_element_type=jnp.float32)
    last[0] = jnp.sum(mixed * cot, axis=0, keepdims=True)
    share(last, m_send, m_recv)
    out_ref[:, final] = (mixed * inverse * gate[heads - 1 : heads, :]).astype(jnp.bfloat16)


    gain_copy.wait_send()
    if D > 1:
        others = tbuf.at[pl.ds(1, D - 1)]
        pltpu.make_async_copy(others, others, t_send).wait()
        others = total.at[pl.ds(1, D - 1)]
        pltpu.make_async_copy(others, others, c_recv).wait()
        pltpu.make_async_copy(others, others, c_send).wait()
    if C > 1:
        others = part.at[pl.ds(1, C - 1)]
        pltpu.make_async_copy(others, others, p_send).wait()

    @pl.loop(0, first)
    def _(h):
        acc = emb[0] * total[0, pl.ds(h, 1), :]
        for j in range(1, D):
            acc = acc + emb[j] * total[j, pl.ds(h, 1), :]
        grad_ref[:, cols(h)] = acc

    def drain(number):
        sent = kv.at[pl.ds(0, number), :, pl.ds(count, (C - 1) * count), :]
        pltpu.make_async_copy(sent, sent, kv_send).wait()
        sent = abuf.at[pl.ds(0, number)]
        pltpu.make_async_copy(sent, sent, a_send).wait()

    fewer = jnp.logical_or(give, swap)

    @pl.when(fewer)
    def _():
        drain(early - 1)

    @pl.when(jnp.logical_not(fewer))
    def _():
        drain(early)

    @pl.when(give)
    def _():
        sent = direct.at[most, :, pl.ds(0, count), :]
        pltpu.make_async_copy(sent, sent, e_send).wait()

    @pl.when(guest)
    def _():
        sent = ubuf.at[pl.ds(0, 3)]
        pltpu.make_async_copy(sent, sent, u_send).wait()

    @pl.when(host)
    def _():
        pltpu.make_async_copy(ures, ures, ur_send).wait()

    @pl.when(take)
    def _():
        sent = direct.at[most, pl.ds(0, 2), pl.ds(count, (C - 1) * count), :]
        pltpu.make_async_copy(sent, sent, ex_send).wait()

    sent = direct.at[pl.ds(0, most), :, pl.ds(0, count), :]
    pltpu.make_async_copy(sent, sent, b_send).wait()
    sent = direct.at[pl.ds(0, most), pl.ds(0, 2), pl.ds(count, (C - 1) * count), :]
    pltpu.make_async_copy(sent, sent, bx_send).wait()

    def grads(rows_of, recv, send, start):
        others = rows_of.at[pl.ds(1, n - 1)]
        pltpu.make_async_copy(others, others, recv).wait()
        sums = []
        for j in range(D):
            acc = rows_of[j]
            for c in range(1, C):
                acc = acc + rows_of[j + c * D]
            sums.append(acc)
        for i in range(rows_of.shape[1]):
            acc = emb[0] * sums[0][i : i + 1, :]
            for j in range(1, D):
                acc = acc + emb[j] * sums[j][i : i + 1, :]
            grad_ref[:, (start + i) * hd : (start + i + 1) * hd] = acc
        pltpu.make_async_copy(others, others, send).wait()

    grads(late, l_recv, l_send, first)
    grads(last, m_recv, m_send, heads - 1)


def store(attn_ref, grad_ref, out_ref, grads_ref, out_sem, grad_sem):
    copies = [
        pltpu.make_async_copy(attn_ref, out_ref, out_sem),
        pltpu.make_async_copy(grad_ref, grads_ref, grad_sem),
    ]
    for copy in copies:
        copy.start()
    for copy in copies:
        copy.wait()


def local(S, C, D, qkv, qk_gain, mod_weight, positions, timesteps, cotangent):
    count, _, width = qkv.shape[2:]
    freqs = mod_weight.shape[1]
    heads = width // HEAD_DIM
    n = C * D
    rows = freqs // n
    hd = HEAD_DIM
    most = DIRECT
    early = heads - most
    first = FIRST
    if S < 3 or C < 2 or D < 2 or early % GROUP or first % GROUP or first + GROUP > early or PAIRED + 2 > early or FORWARD_AT >= early:
        raise ValueError("unsupported mesh")
    bf, f32 = jnp.bfloat16, jnp.float32
    vmem = pl.BlockSpec(memory_space=pltpu.VMEM)
    hbm = pl.BlockSpec(memory_space=pltpu.HBM)
    dma = pltpu.SemaphoreType.DMA
    regular = pltpu.SemaphoreType.REGULAR
    pin = functools.partial(pltpu.with_memory_space_constraint, memory_space=pltpu.HBM)
    attn, grad = pl.pallas_call(
        functools.partial(body, S, C, D, heads, freqs),
        out_shape=(
            jax.ShapeDtypeStruct((count, width), bf),
            jax.ShapeDtypeStruct((rows, width), f32),
        ),
        in_specs=[hbm] * 4 + [pl.BlockSpec(memory_space=pltpu.SMEM), hbm],
        out_specs=(vmem, vmem),
        scratch_shapes=[
            pltpu.VMEM((2, count, width), bf),
            pltpu.VMEM((freqs, width), f32),
            pltpu.VMEM((count, width), bf),
            pltpu.VMEM((heads, 2, C * count, hd), bf),
            pltpu.VMEM((heads, count, hd), bf),
            pltpu.VMEM((heads, count, hd), bf),
            pltpu.VMEM((heads, count, hd), bf),
            pltpu.VMEM((most + 1, 3, C * count, hd), bf),
            pltpu.VMEM((2, width), f32),
            pltpu.VMEM((1, count), jnp.int32),
            pltpu.VMEM((D, 8, hd), f32),
            pltpu.VMEM((-(-heads // 8) * 8, hd), f32),
            pltpu.VMEM((D, rows, hd), f32),
            pltpu.VMEM((count, hd), f32),
            pltpu.VMEM((count, hd), f32),
            pltpu.VMEM((C, first, hd), f32),
            pltpu.VMEM((D, first, hd), f32),
            pltpu.VMEM((n, heads - 1 - first, hd), f32),
            pltpu.VMEM((n, 1, hd), f32),
            pltpu.VMEM((4, count, hd), bf),
            pltpu.VMEM((2, count, hd), bf),
            dma((5,)), dma,
            dma, dma((early - PAIRED // 2,)), dma, dma((early // GROUP,)),
            dma, dma, dma, dma, dma, dma, dma, dma, dma, dma, dma, dma,
            dma, dma, dma, dma((most + 1,)), dma, dma, dma, dma, dma, dma, dma,
            regular, regular, regular, regular, regular,
        ],
        compiler_params=pltpu.CompilerParams(
            collective_id=0, has_side_effects=True, vmem_limit_bytes=VMEM_LIMIT if C <= 2 else 60 << 20
        ),
    )(
        pin(jnp.moveaxis(qkv[0, 0], 1, 0)),
        pin(qk_gain[0]),
        pin(mod_weight[0]),
        pin(positions),
        timesteps,
        pin(cotangent[0, 0]),
    )
    anywhere = pl.BlockSpec(memory_space=pl.ANY)
    attn_out, gate_grad = pl.pallas_call(
        store,
        out_shape=(
            jax.ShapeDtypeStruct((count, width), bf),
            jax.ShapeDtypeStruct((rows, width), f32),
        ),
        in_specs=[anywhere, anywhere],
        out_specs=(anywhere, anywhere),
        scratch_shapes=[dma, dma],
        compiler_params=pltpu.CompilerParams(vmem_limit_bytes=4 << 20),
    )(attn, grad)
    return attn_out[None, None], gate_grad[None]


def solution(mesh):
    sizes = mesh.shape
    return jax.shard_map(
        functools.partial(local, sizes["segment"], sizes["ctx"], sizes["dp"]),
        mesh=mesh,
        in_specs=(
            P("segment", "dp", "ctx", None, None),
            P("segment", None, None),
            P("segment", None, None),
            P("dp", "ctx"),
            P("segment", "dp"),
            P("segment", "dp", "ctx", None),
        ),
        out_specs=(P("segment", "dp", "ctx", None), P("segment", ("ctx", "dp"), None)),
        check_vma=False,
    )
```
